128 devices in a mesh: sky: 16 (over y, x), tm: 8 (over z, core).
Axes of the slice: x: 4, y: 4, z: 4, core: 2. Of those that a mesh axis runs over, the one named last changes fastest.
Arguments:
- reference_spectra: float32 [524288, 64], P('sky'), may hold values from -6 to 6
- observed: float32 [16, 131072, 64], P('sky', 'tm'), may hold values from -6 to 6
- epoch_time: float32 [16, 131072], P('sky', 'tm'), may hold values from -1 to 1
- owner: int32 [16, 131072, 1], P('sky', 'tm'), may hold values from 0 to 15; in each aligned block of 16384 rows (0 to 16383, 16384 to 32767, ..., all dimensions but the last counted through in order) at most 4096 rows name the same one
- source_row: int32 [16, 131072], P('sky', 'tm'), may hold values from 0 to 32767
- unit: int32 [16, 131072, 1], P('sky', 'tm'), may hold values from 0 to 31, as said below
Outputs:
- factor: float32 [16, 32, 192, 192], P('sky', 'tm')
The draws below stay inside these ranges and needn't reach their ends.
Inputs may be any that keep to these rules, and one draw needn't show every extreme that they name: `owner`: among the epochs of one device, at most 4096 name any one sky region, and on some device one region is named by exactly 4096. Among the epochs of one device, every unit has at least 256 and at most 1024 of them; some unit has exactly 256 and some unit exactly 1024.
All inputs are finite; a program needn't handle non-finite values.
Results may differ from the reference program's by a relative error of at most 0.0003.
Values sent between devices are 32-bit elements; how exact they have to be, the bound alone decides.
A program may use at most 256 MiB of HBM per device.

```python
import math
import jax
import jax.numpy as jnp
import numpy as np
from jax import lax

COEFFS = 64
UNITS = 32
E_DEV = 16384
SRC_DEV = 32768
COLUMNS = 192
CAP = 4096
UCAP = 1024
INTERVALS = 16
EPOCHS = 131072
SOURCES = 524288
N_SKY = 16
N_TM = 8


def unit_block(key):
    fewest = E_DEV // (2 * UNITS)
    extra_most = UCAP - fewest
    spare = E_DEV - UNITS * fewest - extra_most
    key_pick, key_pool, key_place = jax.random.split(key, 3)
    chosen = jax.random.permutation(key_pick, jnp.arange(UNITS, dtype=jnp.int32)).astype(jnp.int32)
    busiest = chosen[0]
    others = chosen[2:]
    pool = jnp.repeat(others, extra_most, total_repeat_length=(UNITS - 2) * extra_most).astype(jnp.int32)
    pool = jax.random.permutation(key_pool, pool)[:spare].astype(jnp.int32)
    base_labels = jnp.tile(jnp.arange(UNITS, dtype=jnp.int32), fewest).astype(jnp.int32)
    top_labels = jnp.zeros((extra_most,), jnp.int32) + busiest
    labels = jnp.concatenate([base_labels, top_labels, pool]).astype(jnp.int32)
    return jax.random.permutation(key_place, labels).astype(jnp.int32)


def draw_unit(key, part):
    block_count = INTERVALS * (EPOCHS // E_DEV)
    block_keys = jax.random.split(jax.random.fold_in(key, 7), block_count)
    labels = jax.vmap(unit_block)(block_keys)
    return labels.reshape(INTERVALS, EPOCHS, 1).astype(jnp.int32)


def plant(result, rng, smallest, top_value):
    dims = result.shape
    spot = [jax.random.randint(jax.random.fold_in(rng, axis), (), 0, dims[axis]) for axis in range(len(dims))]
    result = result.at[tuple(spot)].set(smallest)
    longest = dims.index(max(dims))
    spot[longest] = (spot[longest] + 1) % dims[longest]
    return result.at[tuple(spot)].set(top_value)


def shard_levels(own_key, extent, cuts, smallest, largest):
    gain = 1.0
    for axis_at, blocks in cuts:
        steps = jax.random.uniform(jax.random.fold_in(jax.random.fold_in(own_key, 6), axis_at), (blocks,), jnp.float32, smallest / len(cuts), largest / len(cuts))
        gain = gain * jnp.repeat(jnp.exp(steps), extent[axis_at] // blocks).reshape((-1,) + (1,) * (len(extent) - 1 - axis_at))
    return gain


def assign_block(rng, own, number, rows, amount, top, most, slope):
    order = jax.random.permutation(rng, amount)
    crowded, ordinary = portions_of(amount, rows * top, most, slope, True), portions_of(amount, rows * top, most, slope, False)
    places = jnp.arange(amount)

    def named(lengths, turn):
        used = int((lengths > 0).sum())
        fixed = max(1, used // 4)
        shifted = fixed + (places - fixed + turn * (used - fixed)) % max(1, amount - fixed)
        return jnp.zeros((amount,), jnp.int32).at[order[jnp.where(places < fixed, places, shifted)]].set(jnp.asarray(lengths, jnp.int32))

    lengths = jnp.where(number % 4 == 0, named(crowded, number // 4), named(ordinary, number - number // 4 - 1))
    mixed = jax.random.permutation(jax.random.fold_in(own, 3), amount)
    giver, receiver = mixed[0:amount // 2 * 2:2], mixed[1:amount // 2 * 2:2]
    margin = jnp.minimum(lengths[giver] - 1, most - lengths[receiver]) // 2
    margin = jnp.where((giver == order[0]) | (receiver == order[0]) | (lengths[receiver] == 0), 0, jnp.maximum(margin, 0))
    shifted = jax.random.randint(jax.random.fold_in(own, 4), (amount // 2,), 0, 1 << 20) % (margin + 1)
    lengths = lengths.at[giver].add(-shifted).at[receiver].add(shifted)
    members = jnp.searchsorted(jnp.cumsum(lengths), jnp.arange(rows * top), side="right").astype(jnp.int32)
    grid = members.reshape(top, rows).T
    grid = grid[jax.random.permutation(jax.random.fold_in(own, 1), rows)]
    turn = jax.random.randint(jax.random.fold_in(own, 2), (rows, 1), 0, top)
    return jnp.take_along_axis(grid, (jnp.arange(top)[None, :] + turn) % top, axis=1)


def portions_of(number_of, total, reach, lean, full):
    weights = [(1 << 20) // math.isqrt(standing ** lean) + 1 for standing in range(1, number_of + 1)]
    largest = reach if full else min(reach, max(-(-total // number_of), total * weights[0] // sum(weights)))
    least = 1 if total - largest >= number_of - 1 else 0
    counts, surplus = [largest] + [least] * (number_of - 1), total - largest - least * (number_of - 1)
    while surplus > 0:
        free = [i for i in range(1, number_of) if counts[i] < largest] or [i for i in range(1, number_of) if counts[i] < reach]
        whole, remaining = sum([weights[i] for i in free]), surplus
        for i in free:
            more = min(reach - counts[i], max(1, remaining * weights[i] // whole), surplus)
            counts[i] = counts[i] + more
            surplus = surplus - more
    return np.array(counts)


def normal_values(stream_key, extent, width, limit, shards=(), kind=jnp.bfloat16):
    level = shard_levels(stream_key, extent, shards, -0.22, 0.18) if shards else 1.0
    array = jax.random.normal(stream_key, extent, jnp.float32) * width * level
    return jnp.minimum(jnp.maximum(array, -limit), limit).astype(kind)


def setup_inputs(seed: int = 0) -> dict:
    streams_of = jax.random.split(jax.random.key(seed), 7)
    reference_spectra = normal_values(streams_of[0], (SOURCES, COEFFS), 1.0, 6.0, ((0, 16),), jnp.float32)
    observed = normal_values(streams_of[1], (INTERVALS, EPOCHS, COEFFS), 1.0, 6.0, ((0, 16), (1, 8)), jnp.float32)
    epoch_time = jnp.clip(jax.random.uniform(streams_of[2], (INTERVALS, EPOCHS), jnp.float32, -1.0, 1.0) * shard_levels(streams_of[2], (INTERVALS, EPOCHS), ((0, 16), (1, 8)), -0.4, 0.0), -1.0, 1.0)
    owner_keys = jax.random.split(jax.random.fold_in(streams_of[3], 1), INTERVALS * EPOCHS // E_DEV)
    owner_turns = jax.random.permutation(jax.random.fold_in(streams_of[3], 3), INTERVALS * EPOCHS // E_DEV)
    owner = jax.vmap(lambda own, number: assign_block(jax.random.fold_in(streams_of[3], 2), own, number, E_DEV, N_SKY, 1, CAP, 2))(owner_keys, owner_turns).reshape((INTERVALS, EPOCHS, 1))
    source_row = plant(jax.random.randint(streams_of[4], (INTERVALS, EPOCHS), 0, SRC_DEV), jax.random.fold_in(streams_of[4], 1), 0, SRC_DEV - 1).astype(jnp.int32)
    unit = draw_unit(jax.random.fold_in(streams_of[6], 71), 0)
    return dict(reference_spectra=reference_spectra, observed=observed, epoch_time=epoch_time, owner=owner, source_row=source_row, unit=unit)


def slot_index(labels, label_count, capacity):
    onehot = (labels[:, None] == jnp.arange(label_count, dtype=jnp.int32)[None, :]).astype(jnp.int32)
    ranking = jnp.sum(jnp.cumsum(onehot, axis=0) * onehot, axis=1) - 1
    return (labels * capacity + ranking).astype(jnp.int32)

def reference(reference_spectra, observed, epoch_time, owner, source_row, unit):
    row_scale = (UNITS / EPOCHS) ** 0.5
    outputs = []
    for interval in range(N_SKY):

        def block_gram(running, block_index):
            first_row = (block_index * E_DEV).astype(jnp.int32)
            owners = lax.dynamic_slice_in_dim(owner[interval, :, 0], first_row, E_DEV)
            src_rows = lax.dynamic_slice_in_dim(source_row[interval], first_row, E_DEV)
            unit_ids = lax.dynamic_slice_in_dim(unit[interval, :, 0], first_row, E_DEV)
            times_local = lax.dynamic_slice_in_dim(epoch_time[interval], first_row, E_DEV)
            observed_local = lax.dynamic_slice_in_dim(observed[interval], first_row, E_DEV, 0)
            source_ids = (owners * SRC_DEV + src_rows).astype(jnp.int32)
            ref_rows = jnp.take(reference_spectra, source_ids, axis=0)
            design = jnp.concatenate([ref_rows, times_local[:, None] * ref_rows, observed_local], axis=1) * row_scale
            placing = slot_index(unit_ids, UNITS, UCAP)
            buffer = jnp.zeros((UNITS * UCAP, COLUMNS), design.dtype).at[placing].set(design)
            buffer = buffer.reshape(UNITS, UCAP, COLUMNS)
            local_gram = jnp.einsum('ucp,ucq->upq', buffer, buffer, precision=lax.Precision.HIGHEST)
            return (running + local_gram, None)
        start = jnp.zeros((UNITS, COLUMNS, COLUMNS), reference_spectra.dtype)
        total_gram, _ = lax.scan(block_gram, start, jnp.arange(N_TM, dtype=jnp.int32))
        lower = jnp.linalg.cholesky(total_gram)
        outputs.append(jnp.swapaxes(lower, 1, 2))
    return jnp.stack(outputs, axis=0)
```

```python
import functools

import jax
import jax.numpy as jnp
from jax import lax
from jax.experimental import pallas as pl
from jax.experimental.pallas import tpu as pltpu
from jax.sharding import PartitionSpec as P

UNITS = 32
COEFFS = 64
UCAP = 1024
SKY = 16
TM = 8
DEVS = SKY * TM
E_DEV = 16384
STRIPE = 256
SLOTS = 192
HALF = SLOTS // 2
LINES = DEVS * HALF
BLOCK = 256
DUMP = UNITS * UCAP
F32 = jnp.float32
BF16 = jnp.bfloat16
I32 = jnp.int32


def dot(a, b, dims, precision=None):
    return lax.dot_general(a, b, (dims, ((), ())), precision=precision, preferred_element_type=F32)


def route_kernel(round_ref, owner_ref, row_ref, unit_ref, req_ref, slot_ref, place_ref, count_ref, acc_ref):
    first = round_ref[0] * SLOTS
    tri_row = lax.broadcasted_iota(I32, (BLOCK, BLOCK + 128), 0)
    tri_col = lax.broadcasted_iota(I32, (BLOCK, BLOCK + 128), 1)
    before = ((tri_row < tri_col) | (tri_col >= BLOCK)).astype(BF16)
    peers = lax.broadcasted_iota(I32, (DEVS, BLOCK), 0)
    units = lax.broadcasted_iota(I32, (UNITS, BLOCK), 0)
    ranks = lax.broadcasted_iota(I32, (SLOTS, BLOCK), 0)
    acc_ref[...] = jnp.zeros_like(acc_ref)

    def pair(ref, b):
        return jnp.concatenate([ref[pl.ds(2 * b, 1), :], ref[pl.ds(2 * b + 1, 1), :]], axis=1)

    def wide(base):
        return jnp.concatenate([base, base], axis=1)

    def step(b, carry):
        base, unit_base = carry
        owner, row, unit = pair(owner_ref, b), pair(row_ref, b), pair(unit_ref, b)
        stripe = row >> 8
        peer = ((stripe & (SKY - 1)) << 3) + (stripe >> 4)
        local = (owner << 8) + (row & (STRIPE - 1))
        hot = peers == peer
        ahead = dot(hot.astype(BF16), before, ((1,), (0,)))
        rank = jnp.sum(jnp.where(hot, ahead[:, :BLOCK] + wide(base), 0.0), axis=0, keepdims=True)
        rank = rank.astype(I32) - first
        active = (rank >= 0) & (rank < SLOTS)
        upper = jnp.where(rank >= HALF, 1, 0)
        slot = upper * LINES + peer * HALF + rank - upper * HALF
        slot = jnp.where(active, slot, 0)
        high = (local >> 6).astype(F32)
        low = (local & 63).astype(F32)
        values = jnp.concatenate([jnp.where(hot, high, 0.0), jnp.where(hot, low, 0.0)], axis=0).astype(BF16)
        put = (ranks == rank).astype(BF16)
        acc_ref[...] += dot(values, put, ((1,), (1,)))
        mine = (units == unit) & active
        unit_ahead = dot(mine.astype(BF16), before, ((1,), (0,)))
        unit_rank = jnp.sum(jnp.where(mine, unit_ahead[:, :BLOCK] + wide(unit_base), 0.0), axis=0, keepdims=True)
        place = jnp.where(active, unit * UCAP + unit_rank.astype(I32), DUMP)
        for half in range(2):
            lanes = slice(half * 128, half * 128 + 128)
            slot_ref[pl.ds(2 * b + half, 1), :] = slot[:, lanes]
            place_ref[pl.ds(2 * b + half, 1), :] = place[:, lanes]
        return base + ahead[:, BLOCK:], unit_base + unit_ahead[:, BLOCK:]

    start = (jnp.zeros((DEVS, 128), F32), jnp.zeros((UNITS, 128), F32))
    base, unit_base = lax.fori_loop(0, E_DEV // BLOCK, step, start, unroll=4)
    count_ref[...] = unit_base.astype(I32)
    more = (jnp.max(base).astype(I32) > first + SLOTS).astype(I32)
    req_ref[:, 0:128] = (acc_ref[0:DEVS, 0:128] * 64.0 + acc_ref[DEVS:, 0:128]).astype(I32)
    tail = (acc_ref[0:DEVS, 128:] * 64.0 + acc_ref[DEVS:, 128:]).astype(I32)
    req_ref[:, 128:] = jnp.concatenate([tail, jnp.zeros((DEVS, 256 - SLOTS), I32) + more], axis=1)


def route(number, owner, row, unit):
    vmem = pl.BlockSpec(memory_space=pltpu.VMEM)
    return pl.pallas_call(
        route_kernel,
        out_shape=(
            jax.ShapeDtypeStruct((DEVS, 256), I32),
            jax.ShapeDtypeStruct((128, 128), I32),
            jax.ShapeDtypeStruct((128, 128), I32),
            jax.ShapeDtypeStruct((UNITS, 128), I32),
        ),
        in_specs=[pl.BlockSpec(memory_space=pltpu.SMEM), vmem, vmem, vmem],
        out_specs=(vmem,) * 4,
        scratch_shapes=[pltpu.VMEM((2 * DEVS, SLOTS), F32)],
        name="route",
    )(number, owner, row, unit)


PEERS_STEP = 16


def serve_kernel(req_ref, tab_ref, out_ref, rows_ref):
    step = pl.program_id(0)

    @pl.when(step == 0)
    def _():
        for region in range(SKY):
            block = tab_ref[region]
            rows_ref[region * STRIPE : (region + 1) * STRIPE, :] = jnp.concatenate([block, block], axis=0).T

    left = lax.broadcasted_iota(I32, (1, 128), 1) < COEFFS

    def peer_rows(k, _):
        peer = step * PEERS_STEP + k
        for j in range(HALF):
            a = req_ref[peer, j]
            b = req_ref[peer, j + HALF]
            out_ref[k, j : j + 1, :] = jnp.where(left, rows_ref[pl.ds(a, 1), :], rows_ref[pl.ds(b, 1), :])
        return _

    lax.fori_loop(0, PEERS_STEP, peer_rows, 0)


def serve(requests, table):
    return pl.pallas_call(
        serve_kernel,
        grid=(DEVS // PEERS_STEP,),
        out_shape=jax.ShapeDtypeStruct((DEVS, HALF, 128), F32),
        in_specs=[
            pl.BlockSpec(memory_space=pltpu.SMEM),
            pl.BlockSpec((SKY, COEFFS, STRIPE), lambda i: (0, 0, 0), pipeline_mode=pl.Buffered(1)),
        ],
        out_specs=pl.BlockSpec((PEERS_STEP, HALF, 128), lambda i: (i, 0, 0)),
        scratch_shapes=[pltpu.VMEM((SKY * STRIPE, 128), F32)],
        name="serve",
    )(requests, table)


JOIN_STEPS = 8
JOIN_BLOCKS = 128 // JOIN_STEPS


def join_kernel(scale, slot_ref, place_ref, count_ref, time_ref, obs_ref, reply_ref, old_ref, out_ref,
                rows_ref, x0_ref, x1_ref, block_ref, sums_ref, sem):
    step = pl.program_id(0)

    @pl.when(step == 0)
    def _():
        copy = pltpu.make_async_copy(reply_ref, rows_ref.at[pl.ds(0, LINES), :], sem)
        copy.start()
        copy.wait()

        def turn(i, _):
            at = pl.multiple_of(i * 256, 256)
            rows_ref[pl.ds(LINES + at, 256), :] = pltpu.roll(rows_ref[pl.ds(at, 256), :], COEFFS, 1)
            return _

        lax.fori_loop(0, LINES // 256, turn, 0)

    left = lax.broadcasted_iota(I32, (1, 128), 1) < COEFFS

    def place_block(k, _):
        b = step * JOIN_BLOCKS + k
        at = pl.multiple_of(k * 128, 128)
        times = jnp.broadcast_to(time_ref[pl.ds(b, 1), :], (COEFFS, 128))
        block_ref[...] = jnp.concatenate([times, obs_ref[:, pl.ds(at, 128)]], axis=0).T
        for j in range(128):
            s = slot_ref[b, j]
            p = place_ref[b, j]
            r = rows_ref[pl.ds(s, 1), :]
            o = block_ref[j : j + 1, :]
            x0_ref[pl.ds(p, 1), :] = jnp.where(left, r, o)
            x1_ref[pl.ds(p, 1), :] = r * o
        return _

    lax.fori_loop(0, JOIN_BLOCKS, place_block, 0)

    @pl.when(step == JOIN_STEPS - 1)
    def _():
        def unit_gram(u, _):
            count = count_ref[u, 0]
            sums_ref[...] = jnp.zeros_like(sums_ref)

            def add(i, _):
                at = pl.multiple_of(u * UCAP + i * 256, 256)
                x = jnp.concatenate([x0_ref[pl.ds(at, 256), :], x1_ref[pl.ds(at, 256), :]], axis=1)
                rows = lax.broadcasted_iota(I32, (256, 256), 0) + i * 256
                x = jnp.where(rows < count, x, 0.0)
                high = x.astype(BF16)
                low = (x - high.astype(F32)).astype(BF16)
                sums_ref[...] += dot(high, jnp.concatenate([high, low], axis=1), ((0,), (0,)))
                return _

            lax.fori_loop(0, (count + 255) // 256, add, 0)
            cross = sums_ref[:, 256:]
            gram = (sums_ref[:, :256] + cross + cross.T) * scale
            turned = pltpu.roll(gram, COEFFS, 1)
            ref = slice(0, 64)
            obs = slice(64, 128)
            tim = slice(128, 192)
            out_ref[u, :, 0:128] = old_ref[u, :, 0:128] + jnp.where(left, gram[ref, 0:128], turned[ref, 128:256])
            out_ref[u, :, 128:256] = old_ref[u, :, 128:256] + jnp.where(left, turned[ref, 128:256], turned[tim, 128:256])
            out_ref[u, :, 256:384] = old_ref[u, :, 256:384] + jnp.where(left, turned[tim, 128:256], gram[obs, 0:128])
            return _

        lax.fori_loop(0, UNITS, unit_gram, 0)


def join(slot, place, count, times, obs, reply, old, scale):
    smem = pl.BlockSpec(memory_space=pltpu.SMEM)
    once = functools.partial(pl.BlockSpec, pipeline_mode=pl.Buffered(1))
    return pl.pallas_call(
        functools.partial(join_kernel, scale),
        grid=(JOIN_STEPS,),
        out_shape=jax.ShapeDtypeStruct((UNITS, COEFFS, 384), F32),
        in_specs=[
            smem,
            smem,
            smem,
            once((128, 128), lambda i: (0, 0)),
            pl.BlockSpec((COEFFS, JOIN_BLOCKS * 128), lambda i: (0, i)),
            pl.BlockSpec(memory_space=pl.ANY),
            once((UNITS, COEFFS, 384), lambda i: (0, 0, 0)),
        ],
        out_specs=once((UNITS, COEFFS, 384), lambda i: (0, 0, 0)),
        scratch_shapes=[
            pltpu.VMEM((2 * LINES, 128), F32),
            pltpu.VMEM((DUMP + 8, 128), F32),
            pltpu.VMEM((DUMP + 8, 128), F32),
            pltpu.VMEM((128, 128), F32),
            pltpu.VMEM((256, 512), F32),
            pltpu.SemaphoreType.DMA,
        ],
        compiler_params=pltpu.CompilerParams(vmem_limit_bytes=62 << 20),
        name="join",
    )(slot, place, count, times, obs, reply, old)


PANEL = 32


def factor_kernel(gram_ref, out_ref, work_ref):
    many = gram_ref.shape[0]
    work_ref[:, 0:64, 0:128] = gram_ref[:, :, 0:128]
    work_ref[:, 0:64, 128:192] = gram_ref[:, :, 128:192]
    work_ref[:, 64:128, 64:128] = gram_ref[:, :, 192:256]
    work_ref[:, 64:128, 128:192] = gram_ref[:, :, 256:320]
    work_ref[:, 128:192, 128:192] = gram_ref[:, :, 320:384]
    work_ref[:, 64:192, 0:64] = jnp.zeros((many, 128, 64), F32)
    work_ref[:, 128:192, 64:128] = jnp.zeros((many, 64, 64), F32)
    row = lax.broadcasted_iota(I32, (many, PANEL, 192), 1)
    col = lax.broadcasted_iota(I32, (many, PANEL, 192), 2)
    thin = lax.broadcasted_iota(I32, (many, PANEL, 1), 1)
    for start in range(0, 192, PANEL):
        panel = work_ref[:, start : start + PANEL, :]
        for k in range(PANEL - 1):
            pivot = 1.0 / panel[:, k : k + 1, start + k : start + k + 1]
            column = panel[:, :, start + k : start + k + 1]
            factor = jnp.where(thin > k, column * pivot, 0.0)
            panel = panel - factor * panel[:, k : k + 1, :]
        diag = jnp.sum(jnp.where(col == row + start, panel, 0.0), axis=2, keepdims=True)
        panel = jnp.where(col >= row + start, panel * (1.0 / jnp.sqrt(diag)), 0.0)
        out_ref[:, start : start + PANEL, :] = panel
        after = start + PANEL
        if after < 192:
            for m in range(many):
                update = dot(panel[m], panel[m], ((0,), (0,)), lax.Precision.HIGHEST)
                work_ref[m, after:, :] = work_ref[m, after:, :] - update[after:, :]


def upper_factor(packed):
    many = packed.shape[0]
    vmem = pl.BlockSpec(memory_space=pltpu.VMEM)
    return pl.pallas_call(
        factor_kernel,
        out_shape=jax.ShapeDtypeStruct((many, 192, 192), F32),
        in_specs=[vmem],
        out_specs=vmem,
        scratch_shapes=[pltpu.VMEM((many, 192, 192), F32)],
        name="factor",
    )(packed)


def per_device(reference_spectra, observed, epoch_time, owner, source_row, unit):
    obs = observed[0].T
    times = epoch_time.reshape(128, 128)
    owners = owner.reshape(128, 128)
    rows = source_row.reshape(128, 128)
    units = unit.reshape(128, 128)
    scale = UNITS / (E_DEV * TM)
    third = SKY * STRIPE
    mine = lax.dynamic_slice_in_dim(reference_spectra.T, lax.axis_index("tm") * third, third, axis=1)
    stripes = mine.reshape(COEFFS, SKY, STRIPE).transpose(1, 0, 2)
    table = lax.all_to_all(stripes, "sky", split_axis=0, concat_axis=0, tiled=True)

    def one_round(state):
        number, _, gram = state
        requests, slot, place, count = route(number, owners, rows, units)
        asked = lax.all_to_all(requests, ("sky", "tm"), split_axis=0, concat_axis=0, tiled=True)
        more = jnp.max(asked[:, 255]) > 0
        replies = lax.all_to_all(serve(asked, table), ("sky", "tm"), split_axis=0, concat_axis=0, tiled=True)
        gram = join(slot, place, count, times, obs, replies.reshape(LINES, 128), gram, scale)
        return number + 1, more, gram

    start = (jnp.zeros((1,), I32), jnp.array(True), jnp.zeros((UNITS, COEFFS, 384), F32))
    _, _, gram = lax.while_loop(lambda state: state[1], one_round, start)
    shared = lax.psum_scatter(gram, "tm", scatter_dimension=0, tiled=True)
    return upper_factor(shared)[None]


def solution(mesh):
    placed = (
        P("sky", None),
        P("sky", "tm", None),
        P("sky", "tm"),
        P("sky", "tm", None),
        P("sky", "tm"),
        P("sky", "tm", None),
    )
    return jax.shard_map(
        per_device,
        mesh=mesh,
        in_specs=placed,
        out_specs=P("sky", "tm", None, None),
        check_vma=False,
    )
```

```python
import functools

import jax
import jax.numpy as jnp
from jax import lax
from jax.experimental import pallas as pl
from jax.experimental.pallas import tpu as pltpu
from jax.sharding import PartitionSpec as P

UNITS = 32
COEFFS = 64
UCAP = 1024
SKY = 16
TM = 8
DEVS = SKY * TM
E_DEV = 16384
STRIPE = 256
SLOTS = 192
HALF = SLOTS // 2
LINES = DEVS * HALF
BLOCK = 256
DUMP = UNITS * UCAP
F32 = jnp.float32
BF16 = jnp.bfloat16
I32 = jnp.int32


def dot(a, b, dims, precision=None):
    return lax.dot_general(a, b, (dims, ((), ())), precision=precision, preferred_element_type=F32)


def route_kernel(round_ref, owner_ref, row_ref, unit_ref, req_ref, slot_ref, place_ref, count_ref, acc_ref):
    first = round_ref[0] * SLOTS
    tri_row = lax.broadcasted_iota(I32, (BLOCK, BLOCK + 128), 0)
    tri_col = lax.broadcasted_iota(I32, (BLOCK, BLOCK + 128), 1)
    before = ((tri_row < tri_col) | (tri_col >= BLOCK)).astype(BF16)
    peers = lax.broadcasted_iota(I32, (DEVS, BLOCK), 0)
    units = lax.broadcasted_iota(I32, (UNITS, BLOCK), 0)
    ranks = lax.broadcasted_iota(I32, (256, BLOCK), 0)
    acc_ref[...] = jnp.zeros_like(acc_ref)

    def pair(ref, b):
        return jnp.concatenate([ref[pl.ds(2 * b, 1), :], ref[pl.ds(2 * b + 1, 1), :]], axis=1)

    def wide(base):
        return jnp.concatenate([base, base], axis=1)

    def step(b, carry):
        base, unit_base = carry
        owner, row, unit = pair(owner_ref, b), pair(row_ref, b), pair(unit_ref, b)
        stripe = row >> 8
        peer = ((stripe & (SKY - 1)) << 3) + (stripe >> 4)
        local = (owner << 8) + (row & (STRIPE - 1))
        hot = peers == peer
        ahead = dot(hot.astype(BF16), before, ((1,), (0,)))
        rank = jnp.sum(jnp.where(hot, ahead[:, :BLOCK] + wide(base), 0.0), axis=0, keepdims=True)
        rank = rank.astype(I32) - first
        active = (rank >= 0) & (rank < SLOTS)
        upper = jnp.where(rank >= HALF, 1, 0)
        slot = upper * LINES + peer * HALF + rank - upper * HALF
        slot = jnp.where(active, slot, 0)
        high = (local >> 6).astype(F32)
        low = (local & 63).astype(F32)
        values = jnp.concatenate([jnp.where(hot, high, 0.0), jnp.where(hot, low, 0.0)], axis=0).astype(BF16)
        put = (ranks == jnp.where(active, rank + upper * (128 - HALF), 256)).astype(BF16)
        acc_ref[...] += dot(values, put, ((1,), (1,)))
        mine = (units == unit) & active
        unit_ahead = dot(mine.astype(BF16), before, ((1,), (0,)))
        unit_rank = jnp.sum(jnp.where(mine, unit_ahead[:, :BLOCK] + wide(unit_base), 0.0), axis=0, keepdims=True)
        place = jnp.where(active, unit * UCAP + unit_rank.astype(I32), DUMP)
        for half in range(2):
            lanes = slice(half * 128, half * 128 + 128)
            slot_ref[pl.ds(2 * b + half, 1), :] = slot[:, lanes]
            place_ref[pl.ds(2 * b + half, 1), :] = place[:, lanes]
        return base + ahead[:, BLOCK:], unit_base + unit_ahead[:, BLOCK:]

    start = (jnp.zeros((DEVS, 128), F32), jnp.zeros((UNITS, 128), F32))
    base, unit_base = lax.fori_loop(0, E_DEV // BLOCK, step, start, unroll=4)
    count_ref[...] = unit_base.astype(I32)
    more = (jnp.max(base).astype(I32) > first + SLOTS).astype(I32)
    first_half = (acc_ref[0:DEVS, 0:128] * 64.0 + acc_ref[DEVS:, 0:128]).astype(I32)
    lanes = lax.broadcasted_iota(I32, (DEVS, 128), 1)
    req_ref[:, 0, :] = jnp.where(lanes < HALF, first_half, more)
    req_ref[:, 1, :] = (acc_ref[0:DEVS, 128:] * 64.0 + acc_ref[DEVS:, 128:]).astype(I32)


def route(number, owner, row, unit):
    vmem = pl.BlockSpec(memory_space=pltpu.VMEM)
    return pl.pallas_call(
        route_kernel,
        out_shape=(
            jax.ShapeDtypeStruct((DEVS, 2, 128), I32),
            jax.ShapeDtypeStruct((128, 128), I32),
            jax.ShapeDtypeStruct((128, 128), I32),
            jax.ShapeDtypeStruct((UNITS, 128), I32),
        ),
        in_specs=[pl.BlockSpec(memory_space=pltpu.SMEM), vmem, vmem, vmem],
        out_specs=(vmem,) * 4,
        scratch_shapes=[pltpu.VMEM((2 * DEVS, 256), F32)],
        cost_estimate=pl.CostEstimate(flops=10_000_000_000, bytes_accessed=1_000_000, transcendentals=0),
        name="route",
    )(number, owner, row, unit)


MESH = pl.DeviceIdType.MESH
TURN = 37


def exchange_kernel(req_ref, tab_ref, out_ref, asked_ref, rows_ref, index_ref, send_ref,
                    ask_send, ask_recv, local, send_sem, recv_sem):
    sky, tm = lax.axis_index("sky"), lax.axis_index("tm")
    me = sky * TM + tm

    def peer_of(k):
        turn = lax.rem(k * TURN, DEVS)
        x = lax.rem(lax.rem(sky, 4) + lax.rem(turn // 8, 4), 4)
        y = lax.rem(sky // 4 + turn // 32, 4)
        z = lax.rem(tm // 2 + lax.rem(turn // 2, 4), 4)
        core = lax.rem(tm + turn, 2)
        return y * 4 + x, z * 2 + core

    barrier = pltpu.get_barrier_semaphore()

    def greet(k, _):
        pl.semaphore_signal(barrier, inc=1, device_id=peer_of(k), device_id_type=MESH)
        return _

    lax.fori_loop(1, DEVS, greet, 0)
    pl.semaphore_wait(barrier, DEVS - 1)

    def ask(k, _):
        s, t = peer_of(k)
        pltpu.make_async_remote_copy(
            src_ref=req_ref.at[s * TM + t], dst_ref=asked_ref.at[me], send_sem=ask_send, recv_sem=ask_recv,
            device_id=(s, t), device_id_type=MESH,
        ).start()
        return _

    lax.fori_loop(1, DEVS, ask, 0)
    pltpu.make_async_copy(req_ref.at[me], asked_ref.at[me], ask_recv).start()

    for region in range(SKY):
        block = tab_ref[region]
        rows_ref[region * STRIPE : (region + 1) * STRIPE, :] = jnp.concatenate([block, block], axis=0).T

    pltpu.make_async_copy(asked_ref, asked_ref, ask_recv).wait()
    into = pltpu.make_async_copy(asked_ref, index_ref, local)
    into.start()
    into.wait()

    left = lax.broadcasted_iota(I32, (1, 128), 1) < COEFFS

    def gather(peer):
        for j in range(HALF):
            a = index_ref[peer, 0, j]
            b = index_ref[peer, 1, j]
            send_ref[peer, j : j + 1, :] = jnp.where(left, rows_ref[pl.ds(a, 1), :], rows_ref[pl.ds(b, 1), :])

    def send(k):
        s, t = peer_of(k)
        pltpu.make_async_remote_copy(
            src_ref=send_ref.at[s * TM + t], dst_ref=out_ref.at[me], send_sem=send_sem, recv_sem=recv_sem,
            device_id=(s, t), device_id_type=MESH,
        ).start()

    def serve(k, _):
        s, t = peer_of(k)
        gather(s * TM + t)

        @pl.when(k > 1)
        def _():
            send(k - 1)

        return 0

    lax.fori_loop(1, DEVS, serve, 0)
    gather(me)
    send(DEVS - 1)
    pltpu.make_async_copy(send_ref.at[me], out_ref.at[me], recv_sem).start()
    pltpu.make_async_copy(req_ref.at[pl.ds(0, DEVS - 1)], req_ref.at[pl.ds(0, DEVS - 1)], ask_send).wait()
    pltpu.make_async_copy(send_ref.at[pl.ds(0, DEVS - 1)], send_ref.at[pl.ds(0, DEVS - 1)], send_sem).wait()
    pltpu.make_async_copy(out_ref, out_ref, recv_sem).wait()


def exchange(requests, table):
    vmem = pl.BlockSpec(memory_space=pltpu.VMEM)
    return pl.pallas_call(
        exchange_kernel,
        out_shape=(
            jax.ShapeDtypeStruct((DEVS, HALF, 128), F32),
            jax.ShapeDtypeStruct((DEVS, 2, 128), I32),
        ),
        in_specs=[vmem, vmem],
        out_specs=(pl.BlockSpec(memory_space=pl.ANY), vmem),
        scratch_shapes=[
            pltpu.VMEM((SKY * STRIPE, 128), F32),
            pltpu.SMEM((DEVS, 2, 128), I32),
            pltpu.VMEM((DEVS, HALF, 128), F32),
        ] + [pltpu.SemaphoreType.DMA] * 5,
        compiler_params=pltpu.CompilerParams(collective_id=0, has_side_effects=True),
        name="exchange",
    )(requests, table)


JOIN_STEPS = 8
JOIN_BLOCKS = 128 // JOIN_STEPS


def join_kernel(scale, slot_ref, place_ref, count_ref, time_ref, obs_ref, reply_ref, old_ref, out_ref,
                rows_ref, x0_ref, x1_ref, block_ref, sums_ref, sem):
    step = pl.program_id(0)

    @pl.when(step == 0)
    def _():
        copy = pltpu.make_async_copy(reply_ref, rows_ref.at[pl.ds(0, LINES), :], sem)
        copy.start()
        copy.wait()

        def turn(i, _):
            at = pl.multiple_of(i * 256, 256)
            rows_ref[pl.ds(LINES + at, 256), :] = pltpu.roll(rows_ref[pl.ds(at, 256), :], COEFFS, 1)
            return _

        lax.fori_loop(0, LINES // 256, turn, 0)

    left = lax.broadcasted_iota(I32, (1, 128), 1) < COEFFS

    def place_block(k, _):
        b = step * JOIN_BLOCKS + k
        at = pl.multiple_of(k * 128, 128)
        times = jnp.broadcast_to(time_ref[pl.ds(b, 1), :], (COEFFS, 128))
        block_ref[...] = jnp.concatenate([times, obs_ref[:, pl.ds(at, 128)]], axis=0).T
        for j in range(128):
            s = slot_ref[b, j]
            p = place_ref[b, j]
            r = rows_ref[pl.ds(s, 1), :]
            o = block_ref[j : j + 1, :]
            x0_ref[pl.ds(p, 1), :] = jnp.where(left, r, o)
            x1_ref[pl.ds(p, 1), :] = r * o
        return _

    lax.fori_loop(0, JOIN_BLOCKS, place_block, 0)

    @pl.when(step == JOIN_STEPS - 1)
    def _():
        def unit_gram(u, _):
            count = count_ref[u, 0]
            sums_ref[...] = jnp.zeros_like(sums_ref)

            def add(i, _):
                at = pl.multiple_of(u * UCAP + i * 256, 256)
                x = jnp.concatenate([x0_ref[pl.ds(at, 256), :], x1_ref[pl.ds(at, 256), :]], axis=1)
                rows = lax.broadcasted_iota(I32, (256, 256), 0) + i * 256
                x = jnp.where(rows < count, x, 0.0)
                high = x.astype(BF16)
                low = (x - high.astype(F32)).astype(BF16)
                sums_ref[...] += dot(high, jnp.concatenate([high, low], axis=1), ((0,), (0,)))
                return _

            lax.fori_loop(0, (count + 255) // 256, add, 0)
            cross = sums_ref[:, 256:]
            gram = (sums_ref[:, :256] + cross + cross.T) * scale
            turned = pltpu.roll(gram, COEFFS, 1)
            ref = slice(0, 64)
            obs = slice(64, 128)
            tim = slice(128, 192)
            out_ref[u, :, 0:128] = old_ref[u, :, 0:128] + jnp.where(left, gram[ref, 0:128], turned[ref, 128:256])
            out_ref[u, :, 128:256] = old_ref[u, :, 128:256] + jnp.where(left, turned[ref, 128:256], turned[tim, 128:256])
            out_ref[u, :, 256:384] = old_ref[u, :, 256:384] + jnp.where(left, turned[tim, 128:256], gram[obs, 0:128])
            return _

        lax.fori_loop(0, UNITS, unit_gram, 0)


def join(slot, place, count, times, obs, reply, old, scale):
    smem = pl.BlockSpec(memory_space=pltpu.SMEM)
    once = functools.partial(pl.BlockSpec, pipeline_mode=pl.Buffered(1))
    return pl.pallas_call(
        functools.partial(join_kernel, scale),
        grid=(JOIN_STEPS,),
        out_shape=jax.ShapeDtypeStruct((UNITS, COEFFS, 384), F32),
        in_specs=[
            smem,
            smem,
            smem,
            once((128, 128), lambda i: (0, 0)),
            pl.BlockSpec((COEFFS, JOIN_BLOCKS * 128), lambda i: (0, i)),
            pl.BlockSpec(memory_space=pl.ANY),
            once((UNITS, COEFFS, 384), lambda i: (0, 0, 0)),
        ],
        out_specs=once((UNITS, COEFFS, 384), lambda i: (0, 0, 0)),
        scratch_shapes=[
            pltpu.VMEM((2 * LINES, 128), F32),
            pltpu.VMEM((DUMP + 8, 128), F32),
            pltpu.VMEM((DUMP + 8, 128), F32),
            pltpu.VMEM((128, 128), F32),
            pltpu.VMEM((256, 512), F32),
            pltpu.SemaphoreType.DMA,
        ],
        compiler_params=pltpu.CompilerParams(vmem_limit_bytes=62 << 20),
        name="join",
    )(slot, place, count, times, obs, reply, old)


PANEL = 32


def factor_kernel(gram_ref, out_ref, work_ref):
    many = gram_ref.shape[0]
    work_ref[:, 0:64, 0:128] = gram_ref[:, :, 0:128]
    work_ref[:, 0:64, 128:192] = gram_ref[:, :, 128:192]
    work_ref[:, 64:128, 64:128] = gram_ref[:, :, 192:256]
    work_ref[:, 64:128, 128:192] = gram_ref[:, :, 256:320]
    work_ref[:, 128:192, 128:192] = gram_ref[:, :, 320:384]
    work_ref[:, 64:192, 0:64] = jnp.zeros((many, 128, 64), F32)
    work_ref[:, 128:192, 64:128] = jnp.zeros((many, 64, 64), F32)
    row = lax.broadcasted_iota(I32, (many, PANEL, 192), 1)
    col = lax.broadcasted_iota(I32, (many, PANEL, 192), 2)
    thin = lax.broadcasted_iota(I32, (many, PANEL, 1), 1)
    for start in range(0, 192, PANEL):
        panel = work_ref[:, start : start + PANEL, :]
        for k in range(PANEL - 1):
            pivot = 1.0 / panel[:, k : k + 1, start + k : start + k + 1]
            column = panel[:, :, start + k : start + k + 1]
            factor = jnp.where(thin > k, column * pivot, 0.0)
            panel = panel - factor * panel[:, k : k + 1, :]
        diag = jnp.sum(jnp.where(col == row + start, panel, 0.0), axis=2, keepdims=True)
        panel = jnp.where(col >= row + start, panel * (1.0 / jnp.sqrt(diag)), 0.0)
        out_ref[:, start : start + PANEL, :] = panel
        after = start + PANEL
        if after < 192:
            for m in range(many):
                update = dot(panel[m], panel[m], ((0,), (0,)), lax.Precision.HIGHEST)
                work_ref[m, after:, :] = work_ref[m, after:, :] - update[after:, :]


def upper_factor(packed):
    many = packed.shape[0]
    vmem = pl.BlockSpec(memory_space=pltpu.VMEM)
    return pl.pallas_call(
        factor_kernel,
        out_shape=jax.ShapeDtypeStruct((many, 192, 192), F32),
        in_specs=[vmem],
        out_specs=vmem,
        scratch_shapes=[pltpu.VMEM((many, 192, 192), F32)],
        name="factor",
    )(packed)


def per_device(reference_spectra, observed, epoch_time, owner, source_row, unit):
    obs = observed[0].T
    times = epoch_time.reshape(128, 128)
    owners = owner.reshape(128, 128)
    rows = source_row.reshape(128, 128)
    units = unit.reshape(128, 128)
    scale = UNITS / (E_DEV * TM)
    third = SKY * STRIPE
    mine = lax.dynamic_slice_in_dim(reference_spectra.T, lax.axis_index("tm") * third, third, axis=1)
    stripes = mine.reshape(COEFFS, SKY, STRIPE).transpose(1, 0, 2)
    table = lax.all_to_all(stripes, "sky", split_axis=0, concat_axis=0, tiled=True)

    def one_round(state):
        number, _, gram, (requests, slot, place, count) = state
        replies, asked = exchange(requests, table)
        more = jnp.max(asked[:, 0, 127]) > 0
        gram = join(slot, place, count, times, obs, replies.reshape(LINES, 128), gram, scale)
        number = number + 1
        plan = lax.cond(
            more,
            lambda: route(number, owners, rows, units),
            lambda: (requests, slot, place, count),
        )
        return number, more, gram, plan

    number = jnp.zeros((1,), I32)
    start = (number, jnp.array(True), jnp.zeros((UNITS, COEFFS, 384), F32), route(number, owners, rows, units))
    gram = lax.while_loop(lambda state: state[1], one_round, start)[2]
    shared = lax.psum_scatter(gram, "tm", scatter_dimension=0, tiled=True)
    return upper_factor(shared)[None]


def solution(mesh):
    placed = (
        P("sky", None),
        P("sky", "tm", None),
        P("sky", "tm"),
        P("sky", "tm", None),
        P("sky", "tm"),
        P("sky", "tm", None),
    )
    return jax.shard_map(
        per_device,
        mesh=mesh,
        in_specs=placed,
        out_specs=P("sky", "tm", None, None),
        check_vma=False,
    )
```

```python
import functools

import jax
import jax.numpy as jnp
from jax import lax
from jax.experimental import pallas as pl
from jax.experimental.pallas import tpu as pltpu
from jax.sharding import PartitionSpec as P

UNITS = 32
COEFFS = 64
UCAP = 1024
SKY = 16
TM = 8
DEVS = SKY * TM
E_DEV = 16384
STRIPE = 256
SLOTS = 192
HALF = SLOTS // 2
LINES = DEVS * HALF
BLOCK = 256
DUMP = UNITS * UCAP
F32 = jnp.float32
BF16 = jnp.bfloat16
I32 = jnp.int32


def dot(a, b, dims, precision=None):
    return lax.dot_general(a, b, (dims, ((), ())), precision=precision, preferred_element_type=F32)


def route_kernel(round_ref, owner_ref, row_ref, unit_ref, req_ref, slot_ref, place_ref, count_ref, acc_ref):
    first = round_ref[0] * SLOTS
    tri_row = lax.broadcasted_iota(I32, (BLOCK, BLOCK + 128), 0)
    tri_col = lax.broadcasted_iota(I32, (BLOCK, BLOCK + 128), 1)
    before = ((tri_row < tri_col) | (tri_col >= BLOCK)).astype(BF16)
    peers = lax.broadcasted_iota(I32, (DEVS, BLOCK), 0)
    units = lax.broadcasted_iota(I32, (UNITS, BLOCK), 0)
    ranks = lax.broadcasted_iota(I32, (256, BLOCK), 0)
    acc_ref[...] = jnp.zeros_like(acc_ref)

    def pair(ref, b):
        return jnp.concatenate([ref[pl.ds(2 * b, 1), :], ref[pl.ds(2 * b + 1, 1), :]], axis=1)

    def wide(base):
        return jnp.concatenate([base, base], axis=1)

    def step(b, carry):
        base, unit_base = carry
        owner, row, unit = pair(owner_ref, b), pair(row_ref, b), pair(unit_ref, b)
        stripe = row >> 8
        peer = ((stripe & (SKY - 1)) << 3) + (stripe >> 4)
        local = (owner << 8) + (row & (STRIPE - 1))
        hot = peers == peer
        ahead = dot(hot.astype(BF16), before, ((1,), (0,)))
        rank = jnp.sum(jnp.where(hot, ahead[:, :BLOCK] + wide(base), 0.0), axis=0, keepdims=True)
        rank = rank.astype(I32) - first
        active = (rank >= 0) & (rank < SLOTS)
        upper = jnp.where(rank >= HALF, 1, 0)
        slot = upper * LINES + peer * HALF + rank - upper * HALF
        slot = jnp.where(active, slot, 0)
        high = (local >> 6).astype(F32)
        low = (local & 63).astype(F32)
        values = jnp.concatenate([jnp.where(hot, high, 0.0), jnp.where(hot, low, 0.0)], axis=0).astype(BF16)
        put = (ranks == jnp.where(active, rank + upper * (128 - HALF), 256)).astype(BF16)
        acc_ref[...] += dot(values, put, ((1,), (1,)))
        mine = (units == unit) & active
        unit_ahead = dot(mine.astype(BF16), before, ((1,), (0,)))
        unit_rank = jnp.sum(jnp.where(mine, unit_ahead[:, :BLOCK] + wide(unit_base), 0.0), axis=0, keepdims=True)
        place = jnp.where(active, unit * UCAP + unit_rank.astype(I32), DUMP)
        for half in range(2):
            lanes = slice(half * 128, half * 128 + 128)
            slot_ref[pl.ds(2 * b + half, 1), :] = slot[:, lanes]
            place_ref[pl.ds(2 * b + half, 1), :] = place[:, lanes]
        return base + ahead[:, BLOCK:], unit_base + unit_ahead[:, BLOCK:]

    start = (jnp.zeros((DEVS, 128), F32), jnp.zeros((UNITS, 128), F32))
    base, unit_base = lax.fori_loop(0, E_DEV // BLOCK, step, start, unroll=4)
    count_ref[...] = unit_base.astype(I32)
    more = (jnp.max(base).astype(I32) > first + SLOTS).astype(I32)
    first_half = (acc_ref[0:DEVS, 0:128] * 64.0 + acc_ref[DEVS:, 0:128]).astype(I32)
    lanes = lax.broadcasted_iota(I32, (DEVS, 128), 1)
    req_ref[:, 0, :] = jnp.where(lanes < HALF, first_half, more)
    req_ref[:, 1, :] = (acc_ref[0:DEVS, 128:] * 64.0 + acc_ref[DEVS:, 128:]).astype(I32)


def route(number, owner, row, unit):
    vmem = pl.BlockSpec(memory_space=pltpu.VMEM)
    return pl.pallas_call(
        route_kernel,
        out_shape=(
            jax.ShapeDtypeStruct((DEVS, 2, 128), I32),
            jax.ShapeDtypeStruct((128, 128), I32),
            jax.ShapeDtypeStruct((128, 128), I32),
            jax.ShapeDtypeStruct((UNITS, 128), I32),
        ),
        in_specs=[pl.BlockSpec(memory_space=pltpu.SMEM), vmem, vmem, vmem],
        out_specs=(vmem,) * 4,
        scratch_shapes=[pltpu.VMEM((2 * DEVS, 256), F32)],
        cost_estimate=pl.CostEstimate(flops=10_000_000_000, bytes_accessed=1_000_000, transcendentals=0),
        name="route",
    )(number, owner, row, unit)


MESH = pl.DeviceIdType.MESH
TURN = 37


def exchange_kernel(req_ref, tab_ref, out_ref, asked_ref, rows_ref, index_ref, send_ref,
                    ask_send, ask_recv, local, send_sem, recv_sem):
    sky, tm = lax.axis_index("sky"), lax.axis_index("tm")
    me = sky * TM + tm

    def peer_of(k):
        turn = lax.rem(k * TURN, DEVS)
        x = lax.rem(lax.rem(sky, 4) + lax.rem(turn // 8, 4), 4)
        y = lax.rem(sky // 4 + turn // 32, 4)
        z = lax.rem(tm // 2 + lax.rem(turn // 2, 4), 4)
        core = lax.rem(tm + turn, 2)
        return y * 4 + x, z * 2 + core

    barrier = pltpu.get_barrier_semaphore()

    def greet(k, _):
        pl.semaphore_signal(barrier, inc=1, device_id=peer_of(k), device_id_type=MESH)
        return _

    lax.fori_loop(1, DEVS, greet, 0)
    pl.semaphore_wait(barrier, DEVS - 1)

    def ask(k, _):
        s, t = peer_of(k)
        pltpu.make_async_remote_copy(
            src_ref=req_ref.at[s * TM + t], dst_ref=asked_ref.at[me], send_sem=ask_send, recv_sem=ask_recv,
            device_id=(s, t), device_id_type=MESH,
        ).start()
        return _

    lax.fori_loop(1, DEVS, ask, 0)
    pltpu.make_async_copy(req_ref.at[me], asked_ref.at[me], ask_recv).start()

    for region in range(SKY):
        block = tab_ref[region]
        rows_ref[region * STRIPE : (region + 1) * STRIPE, :] = jnp.concatenate([block, block], axis=0).T

    pltpu.make_async_copy(asked_ref, asked_ref, ask_recv).wait()
    into = pltpu.make_async_copy(asked_ref, index_ref, local)
    into.start()
    into.wait()

    left = lax.broadcasted_iota(I32, (1, 128), 1) < COEFFS

    def gather(peer):
        for j in range(HALF):
            a = index_ref[peer, 0, j]
            b = index_ref[peer, 1, j]
            send_ref[peer, j : j + 1, :] = jnp.where(left, rows_ref[pl.ds(a, 1), :], rows_ref[pl.ds(b, 1), :])

    def send(k):
        s, t = peer_of(k)
        pltpu.make_async_remote_copy(
            src_ref=send_ref.at[s * TM + t], dst_ref=out_ref.at[me], send_sem=send_sem, recv_sem=recv_sem,
            device_id=(s, t), device_id_type=MESH,
        ).start()

    def serve(k, _):
        s, t = peer_of(k)
        gather(s * TM + t)

        @pl.when(k > 1)
        def _():
            send(k - 1)

        return 0

    lax.fori_loop(1, DEVS, serve, 0)
    gather(me)
    send(DEVS - 1)
    pltpu.make_async_copy(send_ref.at[me], out_ref.at[me], recv_sem).start()
    pltpu.make_async_copy(req_ref.at[pl.ds(0, DEVS - 1)], req_ref.at[pl.ds(0, DEVS - 1)], ask_send).wait()
    pltpu.make_async_copy(send_ref.at[pl.ds(0, DEVS - 1)], send_ref.at[pl.ds(0, DEVS - 1)], send_sem).wait()
    pltpu.make_async_copy(out_ref, out_ref, recv_sem).wait()


def exchange(requests, table):
    vmem = pl.BlockSpec(memory_space=pltpu.VMEM)
    return pl.pallas_call(
        exchange_kernel,
        out_shape=(
            jax.ShapeDtypeStruct((DEVS, HALF, 128), F32),
            jax.ShapeDtypeStruct((DEVS, 2, 128), I32),
        ),
        in_specs=[vmem, vmem],
        out_specs=(pl.BlockSpec(memory_space=pl.ANY), vmem),
        scratch_shapes=[
            pltpu.VMEM((SKY * STRIPE, 128), F32),
            pltpu.SMEM((DEVS, 2, 128), I32),
            pltpu.VMEM((DEVS, HALF, 128), F32),
        ] + [pltpu.SemaphoreType.DMA] * 5,
        compiler_params=pltpu.CompilerParams(collective_id=0, has_side_effects=True),
        name="exchange",
    )(requests, table)


JOIN_STEPS = 8
JOIN_BLOCKS = 128 // JOIN_STEPS


def join_kernel(scale, slot_ref, place_ref, count_ref, time_ref, obs_ref, reply_ref, old_ref, out_ref,
                rows_ref, x0_ref, x1_ref, block_ref, sums_ref, sem):
    step = pl.program_id(0)

    @pl.when(step == 0)
    def _():
        copy = pltpu.make_async_copy(reply_ref, rows_ref.at[pl.ds(0, LINES), :], sem)
        copy.start()
        copy.wait()

        def turn(i, _):
            at = pl.multiple_of(i * 256, 256)
            rows_ref[pl.ds(LINES + at, 256), :] = pltpu.roll(rows_ref[pl.ds(at, 256), :], COEFFS, 1)
            return _

        lax.fori_loop(0, LINES // 256, turn, 0)

    left = lax.broadcasted_iota(I32, (1, 128), 1) < COEFFS

    def place_block(k, _):
        b = step * JOIN_BLOCKS + k
        at = pl.multiple_of(k * 128, 128)
        times = jnp.broadcast_to(time_ref[pl.ds(b, 1), :], (COEFFS, 128))
        block_ref[...] = jnp.concatenate([times, obs_ref[:, pl.ds(at, 128)]], axis=0).T
        for j in range(128):
            s = slot_ref[b, j]
            p = place_ref[b, j]
            r = rows_ref[pl.ds(s, 1), :]
            o = block_ref[j : j + 1, :]
            x0_ref[pl.ds(p, 1), :] = jnp.where(left, r, o)
            x1_ref[pl.ds(p, 1), :] = r * o
        return _

    lax.fori_loop(0, JOIN_BLOCKS, place_block, 0)

    @pl.when(step == JOIN_STEPS - 1)
    def _():
        def unit_gram(u, _):
            count = count_ref[u, 0]
            sums_ref[...] = jnp.zeros_like(sums_ref)

            def add(i, _):
                at = pl.multiple_of(u * UCAP + i * 256, 256)
                x = jnp.concatenate([x0_ref[pl.ds(at, 256), :], x1_ref[pl.ds(at, 256), :]], axis=1)
                rows = lax.broadcasted_iota(I32, (256, 256), 0) + i * 256
                x = jnp.where(rows < count, x, 0.0)
                high = x.astype(BF16)
                low = (x - high.astype(F32)).astype(BF16)
                sums_ref[...] += dot(high, jnp.concatenate([high, low], axis=1), ((0,), (0,)))
                return _

            lax.fori_loop(0, (count + 255) // 256, add, 0)
            cross = sums_ref[:, 256:]
            gram = (sums_ref[:, :256] + cross + cross.T) * scale
            turned = pltpu.roll(gram, COEFFS, 1)
            ref = slice(0, 64)
            obs = slice(64, 128)
            tim = slice(128, 192)
            out_ref[u, :, 0:128] = old_ref[u, :, 0:128] + jnp.where(left, gram[ref, 0:128], turned[ref, 128:256])
            out_ref[u, :, 128:256] = old_ref[u, :, 128:256] + jnp.where(left, turned[ref, 128:256], turned[tim, 128:256])
            out_ref[u, :, 256:384] = old_ref[u, :, 256:384] + jnp.where(left, turned[tim, 128:256], gram[obs, 0:128])
            return _

        lax.fori_loop(0, UNITS, unit_gram, 0)


def join(slot, place, count, times, obs, reply, old, scale):
    smem = pl.BlockSpec(memory_space=pltpu.SMEM)
    once = functools.partial(pl.BlockSpec, pipeline_mode=pl.Buffered(1))
    return pl.pallas_call(
        functools.partial(join_kernel, scale),
        grid=(JOIN_STEPS,),
        out_shape=jax.ShapeDtypeStruct((UNITS, COEFFS, 384), F32),
        in_specs=[
            smem,
            smem,
            smem,
            once((128, 128), lambda i: (0, 0)),
            pl.BlockSpec((COEFFS, JOIN_BLOCKS * 128), lambda i: (0, i)),
            pl.BlockSpec(memory_space=pl.ANY),
            once((UNITS, COEFFS, 384), lambda i: (0, 0, 0)),
        ],
        out_specs=once((UNITS, COEFFS, 384), lambda i: (0, 0, 0)),
        scratch_shapes=[
            pltpu.VMEM((2 * LINES, 128), F32),
            pltpu.VMEM((DUMP + 8, 128), F32),
            pltpu.VMEM((DUMP + 8, 128), F32),
            pltpu.VMEM((128, 128), F32),
            pltpu.VMEM((256, 512), F32),
            pltpu.SemaphoreType.DMA,
        ],
        compiler_params=pltpu.CompilerParams(vmem_limit_bytes=62 << 20),
        name="join",
    )(slot, place, count, times, obs, reply, old)


PANEL = 32
QUAD = UNITS // TM


def factor(gram, out_ref, work_ref):
    work_ref[...] = jnp.zeros_like(work_ref)
    work_ref[:, 0:64, 0:192] = gram[:, :, 0:192]
    work_ref[:, 64:128, 64:192] = gram[:, :, 192:320]
    work_ref[:, 128:192, 128:192] = gram[:, :, 320:384]
    row = lax.broadcasted_iota(I32, (PANEL, 256), 0)
    col = lax.broadcasted_iota(I32, (PANEL, 256), 1)
    thin = lax.broadcasted_iota(I32, (PANEL, 1), 0)

    def step(i, _):
        at = pl.multiple_of(i * PANEL, PANEL)
        panels = [pltpu.roll(work_ref[m, pl.ds(at, PANEL), :], 256 - at, 1) for m in range(QUAD)]
        for k in range(PANEL - 1):
            for m in range(QUAD):
                panel = panels[m]
                pivot = 1.0 / panel[k : k + 1, k : k + 1]
                below = jnp.where(thin > k, panel[:, k : k + 1] * pivot, 0.0)
                panels[m] = panel - below * panel[k : k + 1, :]
        for m in range(QUAD):
            panel = panels[m]
            diag = jnp.sum(jnp.where(col == row, panel, 0.0), axis=1, keepdims=True)
            panel = jnp.where((col >= row) & (col < 192 - at), panel * (1.0 / jnp.sqrt(diag)), 0.0)
            panel = pltpu.roll(panel, at, 1)
            out_ref[m, pl.ds(at, PANEL), :] = panel[:, :192]
            update = dot(panel, panel, ((0,), (0,)), lax.Precision.HIGHEST)
            work_ref[m] = work_ref[m] - update[:192, :]
        return _

    lax.fori_loop(0, 192 // PANEL, step, 0)


def reduce_kernel(gram_ref, out_ref, pair_ref, sum_ref, part_ref, relay_ref, work_ref,
                  pair_send, pair_recv, ring_send, ring_recv):
    sky, tm = lax.axis_index("sky"), lax.axis_index("tm")
    z, core = tm // 2, lax.rem(tm, 2)
    up, down, far = lax.rem(z + 1, 4), lax.rem(z + 3, 4), lax.rem(z + 2, 4)
    partner = (sky, z * 2 + 1 - core)
    above, below = (sky, up * 2 + core), (sky, down * 2 + core)

    barrier = pltpu.get_barrier_semaphore()
    for other in (partner, above, below):
        pl.semaphore_signal(barrier, inc=1, device_id=other, device_id_type=MESH)
    pl.semaphore_wait(barrier, 3)

    pairs = []
    for n, at in enumerate((far, up, down, z)):
        copy = pltpu.make_async_remote_copy(
            src_ref=gram_ref.at[at * 2 + 1 - core], dst_ref=pair_ref.at[at],
            send_sem=pair_send.at[n], recv_sem=pair_recv.at[n], device_id=partner, device_id_type=MESH,
        )
        copy.start()
        pairs.append(copy)

    def join_pair(n, at):
        pairs[n].wait_recv()
        sum_ref[at] = gram_ref[at * 2 + core] + pair_ref[at]

    def ring(n, src, to):
        copy = pltpu.make_async_remote_copy(
            src_ref=src, dst_ref=part_ref.at[n],
            send_sem=ring_send.at[n], recv_sem=ring_recv.at[n], device_id=to, device_id_type=MESH,
        )
        copy.start()
        return copy

    first, second = pl.ds(0, 2), pl.ds(2, 2)
    join_pair(0, far)
    far_up = ring(0, sum_ref.at[far, first], above)
    far_down = ring(1, sum_ref.at[far, second], below)
    join_pair(1, up)
    near_up = ring(2, sum_ref.at[up, second], above)
    join_pair(2, down)
    near_down = ring(3, sum_ref.at[down, first], below)
    far_up.wait_recv()
    relay_ref[0] = part_ref[0] + sum_ref[up, 0:2]
    last_up = ring(4, relay_ref.at[0], above)
    far_down.wait_recv()
    relay_ref[1] = part_ref[1] + sum_ref[down, 2:4]
    last_down = ring(5, relay_ref.at[1], below)
    join_pair(3, z)
    near_down.wait_recv()
    near_up.wait_recv()
    sum_ref[z, 0:2] = sum_ref[z, 0:2] + part_ref[3]
    sum_ref[z, 2:4] = sum_ref[z, 2:4] + part_ref[2]
    last_up.wait_recv()
    last_down.wait_recv()
    total = jnp.concatenate([sum_ref[z, 0:2] + part_ref[4], sum_ref[z, 2:4] + part_ref[5]], axis=0)
    for copy in (*pairs, far_up, far_down, near_up, near_down, last_up, last_down):
        copy.wait_send()
    factor(total, out_ref, work_ref)


def reduce_factor(gram):
    vmem = pl.BlockSpec(memory_space=pltpu.VMEM)
    return pl.pallas_call(
        reduce_kernel,
        out_shape=jax.ShapeDtypeStruct((QUAD, 192, 192), F32),
        in_specs=[vmem],
        out_specs=vmem,
        scratch_shapes=[
            pltpu.VMEM((4, QUAD, COEFFS, 384), F32),
            pltpu.VMEM((4, QUAD, COEFFS, 384), F32),
            pltpu.VMEM((6, 2, COEFFS, 384), F32),
            pltpu.VMEM((2, 2, COEFFS, 384), F32),
            pltpu.VMEM((QUAD, 192, 256), F32),
            pltpu.SemaphoreType.DMA((4,)),
            pltpu.SemaphoreType.DMA((4,)),
            pltpu.SemaphoreType.DMA((6,)),
            pltpu.SemaphoreType.DMA((6,)),
        ],
        compiler_params=pltpu.CompilerParams(collective_id=1, has_side_effects=True),
        name="reduce_factor",
    )(gram.reshape(TM, QUAD, COEFFS, 384))


def per_device(reference_spectra, observed, epoch_time, owner, source_row, unit):
    obs = observed[0].T
    times = epoch_time.reshape(128, 128)
    owners = owner.reshape(128, 128)
    rows = source_row.reshape(128, 128)
    units = unit.reshape(128, 128)
    scale = UNITS / (E_DEV * TM)
    third = SKY * STRIPE
    mine = lax.dynamic_slice_in_dim(reference_spectra.T, lax.axis_index("tm") * third, third, axis=1)
    stripes = mine.reshape(COEFFS, SKY, STRIPE).transpose(1, 0, 2)
    table = lax.all_to_all(stripes, "sky", split_axis=0, concat_axis=0, tiled=True)

    def one_round(state):
        number, _, gram, (requests, slot, place, count) = state
        replies, asked = exchange(requests, table)
        more = jnp.max(asked[:, 0, 127]) > 0
        gram = join(slot, place, count, times, obs, replies.reshape(LINES, 128), gram, scale)
        number = number + 1
        plan = lax.cond(
            more,
            lambda: route(number, owners, rows, units),
            lambda: (requests, slot, place, count),
        )
        return number, more, gram, plan

    number = jnp.zeros((1,), I32)
    start = (number, jnp.array(True), jnp.zeros((UNITS, COEFFS, 384), F32), route(number, owners, rows, units))
    gram = lax.while_loop(lambda state: state[1], one_round, start)[2]
    return reduce_factor(gram)[None]


def solution(mesh):
    placed = (
        P("sky", None),
        P("sky", "tm", None),
        P("sky", "tm"),
        P("sky", "tm", None),
        P("sky", "tm"),
        P("sky", "tm", None),
    )
    return jax.shard_map(
        per_device,
        mesh=mesh,
        in_specs=placed,
        out_specs=P("sky", "tm", None, None),
        check_vma=False,
    )
```

```python
import functools

import jax
import jax.numpy as jnp
from jax import lax
from jax.experimental import pallas as pl
from jax.experimental.pallas import tpu as pltpu
from jax.sharding import PartitionSpec as P

UNITS = 32
COEFFS = 64
UCAP = 1024
SKY = 16
TM = 8
DEVS = SKY * TM
E_DEV = 16384
STRIPE = 512
CLASSES = DEVS // 2
SLOTS = 352
HALF = SLOTS // 2
LINES = CLASSES * HALF
BLOCK = 256
DUMP = UNITS * UCAP
F32 = jnp.float32
BF16 = jnp.bfloat16
I32 = jnp.int32


def dot(a, b, dims, precision=None):
    return lax.dot_general(a, b, (dims, ((), ())), precision=precision, preferred_element_type=F32)


def route_body(round_ref, owner_ref, row_ref, unit_ref, req_ref, slot_ref, place_ref, count_ref, acc_ref):
    first = round_ref[0] * SLOTS
    tri_row = lax.broadcasted_iota(I32, (BLOCK, BLOCK + 128), 0)
    tri_col = lax.broadcasted_iota(I32, (BLOCK, BLOCK + 128), 1)
    before = ((tri_row < tri_col) | (tri_col >= BLOCK)).astype(BF16)
    classes = lax.broadcasted_iota(I32, (CLASSES, BLOCK), 0)
    units = lax.broadcasted_iota(I32, (UNITS, BLOCK), 0)
    ranks = lax.broadcasted_iota(I32, (SLOTS, BLOCK), 0)
    acc_ref[...] = jnp.zeros_like(acc_ref)

    def pair(ref, b):
        return jnp.concatenate([ref[pl.ds(2 * b, 1), :], ref[pl.ds(2 * b + 1, 1), :]], axis=1)

    def wide(base):
        return jnp.concatenate([base, base], axis=1)

    def step(b, carry):
        base, unit_base = carry
        owner, row, unit = pair(owner_ref, b), pair(row_ref, b), pair(unit_ref, b)
        group = row >> 9
        local = (owner << 9) + (row & (STRIPE - 1))
        hot = classes == group
        ahead = dot(hot.astype(BF16), before, ((1,), (0,)))
        rank = jnp.sum(jnp.where(hot, ahead[:, :BLOCK] + wide(base), 0.0), axis=0, keepdims=True)
        rank = rank.astype(I32) - first
        active = (rank >= 0) & (rank < SLOTS)
        upper = jnp.where(rank >= HALF, 1, 0)
        slot = upper * LINES + group * HALF + rank - upper * HALF
        slot = jnp.where(active, slot, 0)
        high = (local >> 6).astype(F32)
        low = (local & 63).astype(F32)
        values = jnp.concatenate([jnp.where(hot, high, 0.0), jnp.where(hot, low, 0.0)], axis=0).astype(BF16)
        put = (ranks == rank).astype(BF16)
        acc_ref[...] += dot(values, put, ((1,), (1,)))
        mine = (units == unit) & active
        unit_ahead = dot(mine.astype(BF16), before, ((1,), (0,)))
        unit_rank = jnp.sum(jnp.where(mine, unit_ahead[:, :BLOCK] + wide(unit_base), 0.0), axis=0, keepdims=True)
        place = jnp.where(active, unit * UCAP + unit_rank.astype(I32), DUMP) * 2
        for half in range(2):
            lanes = slice(half * 128, half * 128 + 128)
            slot_ref[pl.ds(2 * b + half, 1), :] = slot[:, lanes]
            place_ref[pl.ds(2 * b + half, 1), :] = place[:, lanes]
        return base + ahead[:, BLOCK:], unit_base + unit_ahead[:, BLOCK:]

    start = (jnp.zeros((CLASSES, 128), F32), jnp.zeros((UNITS, 128), F32))
    base, unit_base = lax.fori_loop(0, E_DEV // BLOCK, step, start, unroll=4)
    count_ref[...] = unit_base.astype(I32)
    more = (jnp.max(base).astype(I32) > first + SLOTS).astype(I32)
    wanted = (acc_ref[0:CLASSES, :] * 64.0 + acc_ref[CLASSES:, :]).astype(I32)
    req_ref[:, 0, :] = wanted[:, 0:128]
    req_ref[:, 1, :] = wanted[:, 128:256]
    req_ref[:, 2, :] = jnp.concatenate([wanted[:, 256:], jnp.zeros((CLASSES, 384 - SLOTS), I32)], axis=1)
    req_ref[:, 3, :] = jnp.zeros((CLASSES, 128), I32) + more


PLAN = (
    jax.ShapeDtypeStruct((CLASSES, 4, 128), I32),
    jax.ShapeDtypeStruct((128, 128), I32),
    jax.ShapeDtypeStruct((128, 128), I32),
    jax.ShapeDtypeStruct((UNITS, 128), I32),
)
SMEM_SPEC = pl.BlockSpec(memory_space=pltpu.SMEM)
VMEM_SPEC = pl.BlockSpec(memory_space=pltpu.VMEM)
ANY_SPEC = pl.BlockSpec(memory_space=pl.ANY)


def route(number, owner, row, unit):
    return pl.pallas_call(
        route_body,
        out_shape=PLAN,
        in_specs=[SMEM_SPEC, VMEM_SPEC, VMEM_SPEC, VMEM_SPEC],
        out_specs=(VMEM_SPEC,) * 4,
        scratch_shapes=[pltpu.VMEM((2 * CLASSES, SLOTS), F32)],
        name="route",
    )(number, owner, row, unit)


MESH = pl.DeviceIdType.MESH
TURN = 11


def position():
    sky, tm = lax.axis_index("sky"), lax.axis_index("tm")
    return lax.rem(sky, 4), sky // 4, tm // 2, lax.rem(tm, 2)


def moved(at, offset, sign=1):
    x, y, z, core = (a + sign * o for a, o in zip(at, offset))
    return lax.rem(x + 4, 4), lax.rem(y + 4, 4), lax.rem(z + 4, 4), lax.rem(core + 2, 2)


def mesh_id(at):
    x, y, z, core = at
    return y * 4 + x, z * 2 + core


def class_of(at):
    x, y, z, core = at
    turned = 2 * (z // 2)
    return (lax.rem(z, 2) * 2 + core) * 16 + lax.rem(y + turned, 4) * 4 + lax.rem(x + turned, 4)


def near_offset(k):
    i = lax.rem((k // 2) * TURN, 32)
    x, y, z = lax.rem(i, 4), lax.rem(i // 4, 4), i // 16
    hops = (x * (4 - x) + 2) // 3 + (y * (4 - y) + 2) // 3 + z
    odd = lax.rem(x, 2) * lax.rem(y, 2)
    flat = jnp.where(y == 2, 1, 0)
    tall = jnp.where(odd == 1, jnp.where(x == y, 0, 1), jnp.where(x == 2, 1, 0))
    tie = jnp.where(z == 0, flat, tall)
    flip = jnp.where(hops > 3, 1, jnp.where(hops == 3, tie, 0))
    return lax.rem(x + 2 * flip, 4), lax.rem(y + 2 * flip, 4), z + 2 * flip, lax.rem(k, 2)


def prepare_kernel(round_ref, owner_ref, row_ref, unit_ref, tab_ref,
                   table_ref, req_ref, slot_ref, place_ref, count_ref, acc_ref, send_sem, recv_sem):
    here = position()
    x, y, z, core = here
    sky = y * 4 + x

    def other(k):
        return lax.rem(x + lax.rem(k, 4), 4), lax.rem(y + k // 4, 4), z, core

    def piece(at):
        return tab_ref.at[:, pl.ds(pl.multiple_of(class_of(at) * STRIPE, STRIPE), STRIPE)]

    barrier = pltpu.get_barrier_semaphore()

    def greet(k, _):
        pl.semaphore_signal(barrier, inc=1, device_id=mesh_id(other(k)), device_id_type=MESH)
        return _

    lax.fori_loop(1, SKY, greet, 0)
    pl.semaphore_wait(barrier, SKY - 1)

    def give(k, _):
        at = other(lax.rem(k * 7, SKY))
        pltpu.make_async_remote_copy(
            src_ref=piece(at), dst_ref=table_ref.at[sky], send_sem=send_sem, recv_sem=recv_sem,
            device_id=mesh_id(at), device_id_type=MESH,
        ).start()
        return _

    lax.fori_loop(1, SKY, give, 0)
    pltpu.make_async_copy(piece(here), table_ref.at[sky], recv_sem).start()
    route_body(round_ref, owner_ref, row_ref, unit_ref, req_ref, slot_ref, place_ref, count_ref, acc_ref)
    pltpu.make_async_copy(table_ref.at[pl.ds(0, SKY - 1)], table_ref.at[pl.ds(0, SKY - 1)], send_sem).wait()
    pltpu.make_async_copy(table_ref, table_ref, recv_sem).wait()


def prepare(number, owner, row, unit, spectra):
    return pl.pallas_call(
        prepare_kernel,
        out_shape=(jax.ShapeDtypeStruct((SKY, COEFFS, STRIPE), F32),) + PLAN,
        in_specs=[SMEM_SPEC, VMEM_SPEC, VMEM_SPEC, VMEM_SPEC, ANY_SPEC],
        out_specs=(VMEM_SPEC,) * 5,
        scratch_shapes=[pltpu.VMEM((2 * CLASSES, SLOTS), F32)] + [pltpu.SemaphoreType.DMA] * 2,
        compiler_params=pltpu.CompilerParams(collective_id=2, has_side_effects=True),
        name="prepare",
    )(number, owner, row, unit, spectra)


def exchange_kernel(req_ref, tab_ref, out_ref, more_ref, rows_ref, asked_ref, flag_ref, index_ref, send_ref,
                    ask_send, ask_recv, flag_send, flag_recv, local, send_sem, recv_sem):
    here = position()
    mine = class_of(here)
    half_turn = (2, 2, 2, 0)

    barrier = pltpu.get_barrier_semaphore()

    def greet(k, _):
        pl.semaphore_signal(barrier, inc=1, device_id=mesh_id(moved(here, near_offset(k))), device_id_type=MESH)
        return _

    def greet_far(k, _):
        at = moved(moved(here, near_offset(k)), half_turn)
        pl.semaphore_signal(barrier, inc=1, device_id=mesh_id(at), device_id_type=MESH)
        return _

    lax.fori_loop(1, CLASSES, greet, 0)
    lax.fori_loop(0, CLASSES, greet_far, 0)
    pl.semaphore_wait(barrier, DEVS - 1)

    def ask(k, _):
        at = moved(here, near_offset(k))
        pltpu.make_async_remote_copy(
            src_ref=req_ref.at[class_of(at)], dst_ref=asked_ref.at[k], send_sem=ask_send, recv_sem=ask_recv,
            device_id=mesh_id(at), device_id_type=MESH,
        ).start()
        return _

    def tell(k, _):
        at = moved(moved(here, near_offset(k)), half_turn)
        pltpu.make_async_remote_copy(
            src_ref=req_ref.at[0], dst_ref=flag_ref.at[k], send_sem=flag_send, recv_sem=flag_recv,
            device_id=mesh_id(at), device_id_type=MESH,
        ).start()
        return _

    lax.fori_loop(1, CLASSES, ask, 0)
    pltpu.make_async_copy(req_ref.at[mine], asked_ref.at[0], ask_recv).start()
    lax.fori_loop(0, CLASSES, tell, 0)

    for region in range(SKY):
        block = tab_ref[region]
        rows_ref[region * STRIPE : (region + 1) * STRIPE, :] = jnp.concatenate([block, block], axis=0).T

    pltpu.make_async_copy(asked_ref, asked_ref, ask_recv).wait()
    into = pltpu.make_async_copy(asked_ref, index_ref, local)
    into.start()
    into.wait()

    left = lax.broadcasted_iota(I32, (1, 128), 1) < COEFFS

    def gather(k):
        for j in range(HALF):
            a = index_ref[k, j // 128, j % 128]
            b = index_ref[k, (j + HALF) // 128, (j + HALF) % 128]
            send_ref[k, j : j + 1, :] = jnp.where(left, rows_ref[pl.ds(a, 1), :], rows_ref[pl.ds(b, 1), :])

    def send(k):
        pltpu.make_async_remote_copy(
            src_ref=send_ref.at[k], dst_ref=out_ref.at[mine], send_sem=send_sem, recv_sem=recv_sem,
            device_id=mesh_id(moved(here, near_offset(k), -1)), device_id_type=MESH,
        ).start()

    def serve(k, _):
        gather(k)

        @pl.when(k > 1)
        def _():
            send(k - 1)

        return 0

    lax.fori_loop(1, CLASSES, serve, 0)
    gather(0)
    send(CLASSES - 1)
    pltpu.make_async_copy(send_ref.at[0], out_ref.at[mine], recv_sem).start()
    most = slice(0, CLASSES - 1)
    pltpu.make_async_copy(asked_ref.at[most], asked_ref.at[most], ask_send).wait()
    pltpu.make_async_copy(flag_ref, flag_ref, flag_send).wait()
    pltpu.make_async_copy(flag_ref, flag_ref, flag_recv).wait()
    more_ref[...] = jnp.maximum(jnp.max(asked_ref[:, 3, :], axis=0, keepdims=True),
                                jnp.max(flag_ref[:, 3, :], axis=0, keepdims=True))
    pltpu.make_async_copy(send_ref.at[most], send_ref.at[most], send_sem).wait()
    pltpu.make_async_copy(out_ref, out_ref, recv_sem).wait()


def exchange(requests, table):
    return pl.pallas_call(
        exchange_kernel,
        out_shape=(
            jax.ShapeDtypeStruct((CLASSES, HALF, 128), F32),
            jax.ShapeDtypeStruct((1, 128), I32),
        ),
        in_specs=[VMEM_SPEC, VMEM_SPEC],
        out_specs=(ANY_SPEC, VMEM_SPEC),
        scratch_shapes=[
            pltpu.VMEM((SKY * STRIPE, 128), F32),
            pltpu.VMEM((CLASSES, 4, 128), I32),
            pltpu.VMEM((CLASSES, 4, 128), I32),
            pltpu.SMEM((CLASSES, 4, 128), I32),
            pltpu.VMEM((CLASSES, HALF, 128), F32),
        ] + [pltpu.SemaphoreType.DMA] * 7,
        compiler_params=pltpu.CompilerParams(collective_id=0, has_side_effects=True),
        name="exchange",
    )(requests, table)


JOIN_STEPS = 8
JOIN_BLOCKS = 128 // JOIN_STEPS


def join_kernel(scale, number_ref, slot_ref, place_ref, count_ref, time_ref, obs_ref, reply_ref, old_ref, out_ref,
                rows_ref, x_ref, block_ref, sums_ref, sem, old_sem):
    step = pl.program_id(0)

    @pl.when(step == 0)
    def _():
        copy = pltpu.make_async_copy(reply_ref, rows_ref.at[pl.ds(0, LINES), :], sem)
        copy.start()

        @pl.when(number_ref[0] == 0)
        def _():
            out_ref[...] = jnp.zeros_like(out_ref)

        @pl.when(number_ref[0] > 0)
        def _():
            before = pltpu.make_async_copy(old_ref, out_ref, old_sem)
            before.start()
            before.wait()

        copy.wait()

        def turn(i, _):
            at = pl.multiple_of(i * 256, 256)
            rows_ref[pl.ds(LINES + at, 256), :] = pltpu.roll(rows_ref[pl.ds(at, 256), :], COEFFS, 1)
            return _

        lax.fori_loop(0, LINES // 256, turn, 0)

    left = lax.broadcasted_iota(I32, (1, 128), 1) < COEFFS

    def place_block(k, _):
        b = step * JOIN_BLOCKS + k
        at = pl.multiple_of(k * 128, 128)
        times = jnp.broadcast_to(time_ref[pl.ds(b, 1), :], (COEFFS, 128))
        plain = jnp.concatenate([jnp.ones((COEFFS, 128), F32), obs_ref[:, pl.ds(at, 128)]], axis=0)
        timed = jnp.concatenate([times, jnp.zeros((COEFFS, 128), F32)], axis=0)
        block_ref[pl.ds(0, 128, stride=2), :] = plain.T
        block_ref[pl.ds(1, 128, stride=2), :] = timed.T
        for j in range(128):
            s = slot_ref[b, j]
            p = place_ref[b, j]
            r = rows_ref[pl.ds(s, 2, stride=0), :]
            o = block_ref[2 * j : 2 * j + 2, :]
            x_ref[pl.ds(p, 2), :] = jnp.where(left, r * o, o)
        return _

    lax.fori_loop(0, JOIN_BLOCKS, place_block, 0)

    @pl.when(step == JOIN_STEPS - 1)
    def _():
        def unit_gram(u, _):
            count = count_ref[u, 0]
            sums_ref[...] = jnp.zeros_like(sums_ref)

            def add(i, _):
                at = pl.multiple_of(u * UCAP + i * 256, 256)
                x = jnp.concatenate(
                    [x_ref[pl.ds(2 * at, 256, stride=2), :], x_ref[pl.ds(2 * at + 1, 256, stride=2), :]], axis=1
                )
                rows = lax.broadcasted_iota(I32, (256, 256), 0) + i * 256
                x = jnp.where(rows < count, x, 0.0)
                high = x.astype(BF16)
                low = (x - high.astype(F32)).astype(BF16)
                sums_ref[...] += dot(high, jnp.concatenate([high, low], axis=1), ((0,), (0,)))
                return _

            lax.fori_loop(0, (count + 255) // 256, add, 0)
            cross = sums_ref[:, 256:]
            gram = (sums_ref[:, :256] + cross + cross.T) * scale
            turned = pltpu.roll(gram, COEFFS, 1)
            ref = slice(0, 64)
            obs = slice(64, 128)
            tim = slice(128, 192)
            out_ref[u, :, 0:128] = out_ref[u, :, 0:128] + jnp.where(left, gram[ref, 0:128], turned[ref, 128:256])
            out_ref[u, :, 128:256] = out_ref[u, :, 128:256] + jnp.where(left, turned[ref, 128:256], turned[tim, 128:256])
            out_ref[u, :, 256:384] = out_ref[u, :, 256:384] + jnp.where(left, turned[tim, 128:256], gram[obs, 0:128])
            return _

        lax.fori_loop(0, UNITS, unit_gram, 0)


def join(number, slot, place, count, times, obs, reply, old, scale):
    smem = pl.BlockSpec(memory_space=pltpu.SMEM)
    once = functools.partial(pl.BlockSpec, pipeline_mode=pl.Buffered(1))
    return pl.pallas_call(
        functools.partial(join_kernel, scale),
        grid=(JOIN_STEPS,),
        out_shape=jax.ShapeDtypeStruct((UNITS, COEFFS, 384), F32),
        in_specs=[
            smem,
            smem,
            smem,
            smem,
            once((128, 128), lambda i: (0, 0)),
            pl.BlockSpec((COEFFS, JOIN_BLOCKS * 128), lambda i: (0, i)),
            ANY_SPEC,
            ANY_SPEC,
        ],
        out_specs=once((UNITS, COEFFS, 384), lambda i: (0, 0, 0)),
        scratch_shapes=[
            pltpu.VMEM((2 * LINES + 8, 128), F32),
            pltpu.VMEM((2 * DUMP + 8, 128), F32),
            pltpu.VMEM((256, 128), F32),
            pltpu.VMEM((256, 512), F32),
            pltpu.SemaphoreType.DMA,
            pltpu.SemaphoreType.DMA,
        ],
        compiler_params=pltpu.CompilerParams(vmem_limit_bytes=62 << 20),
        name="join",
    )(number, slot, place, count, times, obs, reply, old)


PANEL = 32
QUAD = UNITS // TM


def factor(gram, out_ref, work_ref):
    work_ref[...] = jnp.zeros_like(work_ref)
    work_ref[:, 0:64, 0:192] = gram[:, :, 0:192]
    work_ref[:, 64:128, 64:192] = gram[:, :, 192:320]
    work_ref[:, 128:192, 128:192] = gram[:, :, 320:384]
    row = lax.broadcasted_iota(I32, (PANEL, 256), 0)
    col = lax.broadcasted_iota(I32, (PANEL, 256), 1)
    thin = lax.broadcasted_iota(I32, (PANEL, 1), 0)

    def step(i, _):
        at = pl.multiple_of(i * PANEL, PANEL)
        panels = [pltpu.roll(work_ref[m, pl.ds(at, PANEL), :], 256 - at, 1) for m in range(QUAD)]
        for k in range(PANEL - 1):
            for m in range(QUAD):
                panel = panels[m]
                pivot = 1.0 / panel[k : k + 1, k : k + 1]
                below = jnp.where(thin > k, panel[:, k : k + 1] * pivot, 0.0)
                panels[m] = panel - below * panel[k : k + 1, :]
        for m in range(QUAD):
            panel = panels[m]
            diag = jnp.sum(jnp.where(col == row, panel, 0.0), axis=1, keepdims=True)
            panel = jnp.where((col >= row) & (col < 192 - at), panel * (1.0 / jnp.sqrt(diag)), 0.0)
            panel = pltpu.roll(panel, at, 1)
            out_ref[m, pl.ds(at, PANEL), :] = panel[:, :192]
            update = dot(panel, panel, ((0,), (0,)), lax.Precision.HIGHEST)
            work_ref[m] = work_ref[m] - update[:192, :]
        return _

    lax.fori_loop(0, 192 // PANEL, step, 0)


def reduce_kernel(gram_ref, out_ref, pair_ref, sum_ref, part_ref, relay_ref, work_ref,
                  pair_send, pair_recv, ring_send, ring_recv):
    sky, tm = lax.axis_index("sky"), lax.axis_index("tm")
    z, core = tm // 2, lax.rem(tm, 2)
    up, down, far = lax.rem(z + 1, 4), lax.rem(z + 3, 4), lax.rem(z + 2, 4)
    partner = (sky, z * 2 + 1 - core)
    above, below = (sky, up * 2 + core), (sky, down * 2 + core)

    barrier = pltpu.get_barrier_semaphore()
    for other in (partner, above, below):
        pl.semaphore_signal(barrier, inc=1, device_id=other, device_id_type=MESH)
    pl.semaphore_wait(barrier, 3)

    pairs = []
    for n, at in enumerate((far, up, down, z)):
        copy = pltpu.make_async_remote_copy(
            src_ref=gram_ref.at[at * 2 + 1 - core], dst_ref=pair_ref.at[at],
            send_sem=pair_send.at[n], recv_sem=pair_recv.at[n], device_id=partner, device_id_type=MESH,
        )
        copy.start()
        pairs.append(copy)

    def join_pair(n, at):
        pairs[n].wait_recv()
        sum_ref[at] = gram_ref[at * 2 + core] + pair_ref[at]

    def ring(n, src, to):
        copy = pltpu.make_async_remote_copy(
            src_ref=src, dst_ref=part_ref.at[n],
            send_sem=ring_send.at[n], recv_sem=ring_recv.at[n], device_id=to, device_id_type=MESH,
        )
        copy.start()
        return copy

    first, second = pl.ds(0, 2), pl.ds(2, 2)
    join_pair(0, far)
    far_up = ring(0, sum_ref.at[far, first], above)
    far_down = ring(1, sum_ref.at[far, second], below)
    join_pair(1, up)
    near_up = ring(2, sum_ref.at[up, second], above)
    join_pair(2, down)
    near_down = ring(3, sum_ref.at[down, first], below)
    far_up.wait_recv()
    relay_ref[0] = part_ref[0] + sum_ref[up, 0:2]
    last_up = ring(4, relay_ref.at[0], above)
    far_down.wait_recv()
    relay_ref[1] = part_ref[1] + sum_ref[down, 2:4]
    last_down = ring(5, relay_ref.at[1], below)
    join_pair(3, z)
    near_down.wait_recv()
    near_up.wait_recv()
    sum_ref[z, 0:2] = sum_ref[z, 0:2] + part_ref[3]
    sum_ref[z, 2:4] = sum_ref[z, 2:4] + part_ref[2]
    last_up.wait_recv()
    last_down.wait_recv()
    total = jnp.concatenate([sum_ref[z, 0:2] + part_ref[4], sum_ref[z, 2:4] + part_ref[5]], axis=0)
    for copy in (*pairs, far_up, far_down, near_up, near_down, last_up, last_down):
        copy.wait_send()
    factor(total, out_ref, work_ref)


def reduce_factor(gram):
    vmem = pl.BlockSpec(memory_space=pltpu.VMEM)
    return pl.pallas_call(
        reduce_kernel,
        out_shape=jax.ShapeDtypeStruct((QUAD, 192, 192), F32),
        in_specs=[vmem],
        out_specs=vmem,
        scratch_shapes=[
            pltpu.VMEM((4, QUAD, COEFFS, 384), F32),
            pltpu.VMEM((4, QUAD, COEFFS, 384), F32),
            pltpu.VMEM((6, 2, COEFFS, 384), F32),
            pltpu.VMEM((2, 2, COEFFS, 384), F32),
            pltpu.VMEM((QUAD, 192, 256), F32),
            pltpu.SemaphoreType.DMA((4,)),
            pltpu.SemaphoreType.DMA((4,)),
            pltpu.SemaphoreType.DMA((6,)),
            pltpu.SemaphoreType.DMA((6,)),
        ],
        compiler_params=pltpu.CompilerParams(collective_id=1, has_side_effects=True),
        name="reduce_factor",
    )(gram.reshape(TM, QUAD, COEFFS, 384))


def per_device(reference_spectra, observed, epoch_time, owner, source_row, unit):
    obs = observed[0].T
    times = epoch_time.reshape(128, 128)
    owners = owner.reshape(128, 128)
    rows = source_row.reshape(128, 128)
    units = unit.reshape(128, 128)
    scale = UNITS / (E_DEV * TM)
    number = jnp.zeros((1,), I32)
    table, *plan = prepare(number, owners, rows, units, reference_spectra.T)

    def one_round(state):
        number, _, gram, plan = state
        requests, slot, place, count = plan
        replies, flags = exchange(requests, table)
        more = flags[0, 0] > 0
        gram = join(number, slot, place, count, times, obs, replies.reshape(LINES, 128), gram, scale)
        number = number + 1
        plan = lax.cond(more, lambda: tuple(route(number, owners, rows, units)), lambda: plan)
        return number, more, gram, plan

    start = (number, jnp.array(True), jnp.zeros((UNITS, COEFFS, 384), F32), tuple(plan))
    gram = lax.while_loop(lambda state: state[1], one_round, start)[2]
    return reduce_factor(gram)[None]


def solution(mesh):
    placed = (
        P("sky", None),
        P("sky", "tm", None),
        P("sky", "tm"),
        P("sky", "tm", None),
        P("sky", "tm"),
        P("sky", "tm", None),
    )
    return jax.shard_map(
        per_device,
        mesh=mesh,
        in_specs=placed,
        out_specs=P("sky", "tm", None, None),
        check_vma=False,
    )
```

```python
import functools

import jax
import jax.numpy as jnp
from jax import lax
from jax.experimental import pallas as pl
from jax.experimental.pallas import tpu as pltpu
from jax.sharding import PartitionSpec as P

UNITS = 32
COEFFS = 64
UCAP = 1024
SKY = 16
TM = 8
DEVS = SKY * TM
E_DEV = 16384
STRIPE = 512
CLASSES = DEVS // 2
SLOTS = 352
HALF = SLOTS // 2
LINES = CLASSES * HALF
BLOCK = 256
DUMP = UNITS * UCAP
F32 = jnp.float32
BF16 = jnp.bfloat16
I32 = jnp.int32


def dot(a, b, dims, precision=None):
    return lax.dot_general(a, b, (dims, ((), ())), precision=precision, preferred_element_type=F32)


def route_body(round_ref, owner_ref, row_ref, unit_ref, req_ref, slot_ref, place_ref, count_ref, acc_ref):
    first = round_ref[0] * SLOTS
    tri_row = lax.broadcasted_iota(I32, (BLOCK, BLOCK + 128), 0)
    tri_col = lax.broadcasted_iota(I32, (BLOCK, BLOCK + 128), 1)
    before = ((tri_row < tri_col) | (tri_col >= BLOCK)).astype(BF16)
    classes = lax.broadcasted_iota(I32, (CLASSES, BLOCK), 0)
    units = lax.broadcasted_iota(I32, (UNITS, BLOCK), 0)
    ranks = lax.broadcasted_iota(I32, (SLOTS, BLOCK), 0)
    acc_ref[...] = jnp.zeros_like(acc_ref)

    def pair(ref, b):
        return jnp.concatenate([ref[pl.ds(2 * b, 1), :], ref[pl.ds(2 * b + 1, 1), :]], axis=1)

    def wide(base):
        return jnp.concatenate([base, base], axis=1)

    def step(b, carry):
        base, unit_base = carry
        owner, row, unit = pair(owner_ref, b), pair(row_ref, b), pair(unit_ref, b)
        group = row >> 9
        local = (owner << 9) + (row & (STRIPE - 1))
        hot = classes == group
        ahead = dot(hot.astype(BF16), before, ((1,), (0,)))
        rank = jnp.sum(jnp.where(hot, ahead[:, :BLOCK] + wide(base), 0.0), axis=0, keepdims=True)
        rank = rank.astype(I32) - first
        active = (rank >= 0) & (rank < SLOTS)
        upper = jnp.where(rank >= HALF, 1, 0)
        slot = upper * LINES + group * HALF + rank - upper * HALF
        slot = jnp.where(active, slot, 0)
        high = (local >> 6).astype(F32)
        low = (local & 63).astype(F32)
        values = jnp.concatenate([jnp.where(hot, high, 0.0), jnp.where(hot, low, 0.0)], axis=0).astype(BF16)
        put = (ranks == rank).astype(BF16)
        acc_ref[...] += dot(values, put, ((1,), (1,)))
        mine = (units == unit) & active
        unit_ahead = dot(mine.astype(BF16), before, ((1,), (0,)))
        unit_rank = jnp.sum(jnp.where(mine, unit_ahead[:, :BLOCK] + wide(unit_base), 0.0), axis=0, keepdims=True)
        place = jnp.where(active, unit * UCAP + unit_rank.astype(I32), DUMP) * 2
        for half in range(2):
            lanes = slice(half * 128, half * 128 + 128)
            slot_ref[pl.ds(2 * b + half, 1), :] = slot[:, lanes]
            place_ref[pl.ds(2 * b + half, 1), :] = place[:, lanes]
        return base + ahead[:, BLOCK:], unit_base + unit_ahead[:, BLOCK:]

    start = (jnp.zeros((CLASSES, 128), F32), jnp.zeros((UNITS, 128), F32))
    base, unit_base = lax.fori_loop(0, E_DEV // BLOCK, step, start, unroll=4)
    count_ref[...] = unit_base.astype(I32)
    more = (jnp.max(base).astype(I32) > first + SLOTS).astype(I32)
    wanted = (acc_ref[0:CLASSES, :] * 64.0 + acc_ref[CLASSES:, :]).astype(I32)
    req_ref[:, 0, :] = wanted[:, 0:128]
    req_ref[:, 1, :] = wanted[:, 128:256]
    req_ref[:, 2, :] = jnp.concatenate([wanted[:, 256:], jnp.zeros((CLASSES, 384 - SLOTS), I32)], axis=1)
    req_ref[:, 3, :] = jnp.zeros((CLASSES, 128), I32) + more


PLAN = (
    jax.ShapeDtypeStruct((CLASSES, 4, 128), I32),
    jax.ShapeDtypeStruct((128, 128), I32),
    jax.ShapeDtypeStruct((128, 128), I32),
    jax.ShapeDtypeStruct((UNITS, 128), I32),
)
SMEM_SPEC = pl.BlockSpec(memory_space=pltpu.SMEM)
VMEM_SPEC = pl.BlockSpec(memory_space=pltpu.VMEM)
ANY_SPEC = pl.BlockSpec(memory_space=pl.ANY)


def route(number, owner, row, unit):
    return pl.pallas_call(
        route_body,
        out_shape=PLAN,
        in_specs=[SMEM_SPEC, VMEM_SPEC, VMEM_SPEC, VMEM_SPEC],
        out_specs=(VMEM_SPEC,) * 4,
        scratch_shapes=[pltpu.VMEM((2 * CLASSES, SLOTS), F32)],
        name="route",
    )(number, owner, row, unit)


MESH = pl.DeviceIdType.MESH
TURN = 11


def nearer(i):
    x, y, z = i % 4, i // 4 % 4, i // 16
    hops = min(x, 4 - x) + min(y, 4 - y) + z
    if hops != 3:
        return int(hops > 3)
    if z == 0:
        return int(y == 2)
    return int(x != y) if x % 2 and y % 2 else int(x == 2)


FLIPS = sum(nearer(i) << i for i in range(32))


def position():
    sky, tm = lax.axis_index("sky"), lax.axis_index("tm")
    return sky & 3, sky >> 2, tm >> 1, tm & 1


def moved(at, offset):
    x, y, z, core = (a + o for a, o in zip(at, offset))
    return x & 3, y & 3, z & 3, core & 1


def mesh_id(at):
    x, y, z, core = at
    return y * 4 + x, z * 2 + core


def class_of(at):
    x, y, z, core = at
    turned = z & 2
    return ((z & 1) * 2 + core) * 16 + ((y + turned) & 3) * 4 + ((x + turned) & 3)


def near_offset(k):
    i = ((k >> 1) * TURN) & 31
    flip = ((FLIPS >> i) & 1) * 2
    return (i & 3) + flip, (i >> 2) + flip, (i >> 4) + flip, k & 1


def next_device(k):
    to = lax.axis_index("sky") * TM + lax.axis_index("tm") + k
    return (to >> 3) & (SKY - 1), to & (TM - 1)


def prepare_kernel(round_ref, owner_ref, row_ref, unit_ref, tab_ref,
                   table_ref, req_ref, slot_ref, place_ref, count_ref, acc_ref, send_sem, recv_sem):
    here = position()
    x, y, z, core = here
    sky = y * 4 + x

    def other(k):
        return (x + k) & 3, (y + (k >> 2)) & 3, z, core

    def piece(at):
        return tab_ref.at[:, pl.ds(pl.multiple_of(class_of(at) * STRIPE, STRIPE), STRIPE)]

    barrier = pltpu.get_barrier_semaphore()

    def greet(k, _):
        pl.semaphore_signal(barrier, inc=1, device_id=mesh_id(other(k)), device_id_type=MESH)
        return _

    lax.fori_loop(1, SKY, greet, 0)
    pl.semaphore_wait(barrier, SKY - 1)

    def give(k, _):
        at = other((k * 7) & (SKY - 1))
        pltpu.make_async_remote_copy(
            src_ref=piece(at), dst_ref=table_ref.at[sky], send_sem=send_sem, recv_sem=recv_sem,
            device_id=mesh_id(at), device_id_type=MESH,
        ).start()
        return _

    lax.fori_loop(1, SKY, give, 0)
    pltpu.make_async_copy(piece(here), table_ref.at[sky], recv_sem).start()
    route_body(round_ref, owner_ref, row_ref, unit_ref, req_ref, slot_ref, place_ref, count_ref, acc_ref)
    pltpu.make_async_copy(table_ref.at[pl.ds(0, SKY - 1)], table_ref.at[pl.ds(0, SKY - 1)], send_sem).wait()
    pltpu.make_async_copy(table_ref, table_ref, recv_sem).wait()


def prepare(number, owner, row, unit, spectra):
    return pl.pallas_call(
        prepare_kernel,
        out_shape=(jax.ShapeDtypeStruct((SKY, COEFFS, STRIPE), F32),) + PLAN,
        in_specs=[SMEM_SPEC, VMEM_SPEC, VMEM_SPEC, VMEM_SPEC, ANY_SPEC],
        out_specs=(VMEM_SPEC,) * 5,
        scratch_shapes=[pltpu.VMEM((2 * CLASSES, SLOTS), F32)] + [pltpu.SemaphoreType.DMA] * 2,
        compiler_params=pltpu.CompilerParams(collective_id=2, has_side_effects=True),
        name="prepare",
    )(number, owner, row, unit, spectra)


def exchange_kernel(req_ref, tab_ref, out_ref, more_ref, rows_ref, asked_ref, flag_ref, index_ref, send_ref,
                    ask_send, ask_recv, flag_send, flag_recv, local, send_sem, recv_sem):
    here = position()
    mine = class_of(here)
    half_turn = (2, 2, 2, 0)

    barrier = pltpu.get_barrier_semaphore()

    def greet(k, _):
        pl.semaphore_signal(barrier, inc=1, device_id=next_device(k), device_id_type=MESH)
        return _

    lax.fori_loop(1, DEVS, greet, 0)
    pl.semaphore_wait(barrier, DEVS - 1)

    def ask(k, _):
        at = moved(here, near_offset(k))
        pltpu.make_async_remote_copy(
            src_ref=req_ref.at[class_of(at)], dst_ref=asked_ref.at[k], send_sem=ask_send, recv_sem=ask_recv,
            device_id=mesh_id(at), device_id_type=MESH,
        ).start()
        return _

    def tell(k, _):
        at = moved(moved(here, near_offset(k)), half_turn)
        pltpu.make_async_remote_copy(
            src_ref=req_ref.at[0], dst_ref=flag_ref.at[k], send_sem=flag_send, recv_sem=flag_recv,
            device_id=mesh_id(at), device_id_type=MESH,
        ).start()
        return _

    lax.fori_loop(1, CLASSES, ask, 0)
    pltpu.make_async_copy(req_ref.at[mine], asked_ref.at[0], ask_recv).start()
    lax.fori_loop(0, CLASSES, tell, 0)

    for region in range(SKY):
        block = tab_ref[region]
        rows_ref[region * STRIPE : (region + 1) * STRIPE, :] = jnp.concatenate([block, block], axis=0).T

    pltpu.make_async_copy(asked_ref, asked_ref, ask_recv).wait()
    into = pltpu.make_async_copy(asked_ref, index_ref, local)
    into.start()
    into.wait()

    left = lax.broadcasted_iota(I32, (1, 128), 1) < COEFFS

    def gather(k):
        for j in range(HALF):
            a = index_ref[k, j // 128, j % 128]
            b = index_ref[k, (j + HALF) // 128, (j + HALF) % 128]
            send_ref[k, j : j + 1, :] = jnp.where(left, rows_ref[pl.ds(a, 1), :], rows_ref[pl.ds(b, 1), :])

    def send(k):
        pltpu.make_async_remote_copy(
            src_ref=send_ref.at[k], dst_ref=out_ref.at[mine], send_sem=send_sem, recv_sem=recv_sem,
            device_id=mesh_id(moved(here, [-o for o in near_offset(k)])), device_id_type=MESH,
        ).start()

    def serve(k, _):
        gather(k)

        @pl.when(k > 1)
        def _():
            send(k - 1)

        return 0

    lax.fori_loop(1, CLASSES, serve, 0)
    gather(0)
    send(CLASSES - 1)
    pltpu.make_async_copy(send_ref.at[0], out_ref.at[mine], recv_sem).start()
    most = slice(0, CLASSES - 1)
    pltpu.make_async_copy(asked_ref.at[most], asked_ref.at[most], ask_send).wait()
    pltpu.make_async_copy(flag_ref, flag_ref, flag_send).wait()
    pltpu.make_async_copy(flag_ref, flag_ref, flag_recv).wait()
    more_ref[...] = jnp.maximum(jnp.max(asked_ref[:, 3, :], axis=0, keepdims=True),
                                jnp.max(flag_ref[:, 3, :], axis=0, keepdims=True))
    pltpu.make_async_copy(send_ref.at[most], send_ref.at[most], send_sem).wait()
    pltpu.make_async_copy(out_ref, out_ref, recv_sem).wait()


def exchange(collective, requests, table):
    return pl.pallas_call(
        exchange_kernel,
        out_shape=(
            jax.ShapeDtypeStruct((CLASSES, HALF, 128), F32),
            jax.ShapeDtypeStruct((1, 128), I32),
        ),
        in_specs=[VMEM_SPEC, VMEM_SPEC],
        out_specs=(ANY_SPEC, VMEM_SPEC),
        scratch_shapes=[
            pltpu.VMEM((SKY * STRIPE, 128), F32),
            pltpu.VMEM((CLASSES, 4, 128), I32),
            pltpu.VMEM((CLASSES, 4, 128), I32),
            pltpu.SMEM((CLASSES, 4, 128), I32),
            pltpu.VMEM((CLASSES, HALF, 128), F32),
        ] + [pltpu.SemaphoreType.DMA] * 7,
        compiler_params=pltpu.CompilerParams(collective_id=collective, has_side_effects=True),
        name="exchange",
    )(requests, table)


JOIN_STEPS = 8
JOIN_BLOCKS = 128 // JOIN_STEPS


def join_kernel(scale, slot_ref, place_ref, count_ref, time_ref, obs_ref, reply_ref, *refs):
    *old_ref, out_ref, rows_ref, x_ref, block_ref, sums_ref, sem, old_sem = refs
    step = pl.program_id(0)

    @pl.when(step == 0)
    def _():
        copy = pltpu.make_async_copy(reply_ref, rows_ref.at[pl.ds(0, LINES), :], sem)
        copy.start()

        for old in old_ref:
            before = pltpu.make_async_copy(old, out_ref, old_sem)
            before.start()
            before.wait()
        copy.wait()

        def turn(i, _):
            at = pl.multiple_of(i * 256, 256)
            rows_ref[pl.ds(LINES + at, 256), :] = pltpu.roll(rows_ref[pl.ds(at, 256), :], COEFFS, 1)
            return _

        lax.fori_loop(0, LINES // 256, turn, 0)

    left = lax.broadcasted_iota(I32, (1, 128), 1) < COEFFS

    def place_block(k, _):
        b = step * JOIN_BLOCKS + k
        at = pl.multiple_of(k * 128, 128)
        times = jnp.broadcast_to(time_ref[pl.ds(b, 1), :], (COEFFS, 128))
        plain = jnp.concatenate([jnp.ones((COEFFS, 128), F32), obs_ref[:, pl.ds(at, 128)]], axis=0)
        timed = jnp.concatenate([times, jnp.zeros((COEFFS, 128), F32)], axis=0)
        block_ref[pl.ds(0, 128, stride=2), :] = plain.T
        block_ref[pl.ds(1, 128, stride=2), :] = timed.T
        for j in range(128):
            s = slot_ref[b, j]
            p = place_ref[b, j]
            r = rows_ref[pl.ds(s, 2, stride=0), :]
            o = block_ref[2 * j : 2 * j + 2, :]
            x_ref[pl.ds(p, 2), :] = jnp.where(left, r * o, o)
        return _

    lax.fori_loop(0, JOIN_BLOCKS, place_block, 0)

    @pl.when(step == JOIN_STEPS - 1)
    def _():
        def put(u, at, value):
            lanes = slice(at, at + 128)
            out_ref[u, :, lanes] = out_ref[u, :, lanes] + value if old_ref else value

        def unit_gram(u, _):
            count = count_ref[u, 0]
            sums_ref[...] = jnp.zeros_like(sums_ref)

            def add(i, _):
                at = pl.multiple_of(u * UCAP + i * 256, 256)
                x = jnp.concatenate(
                    [x_ref[pl.ds(2 * at, 256, stride=2), :], x_ref[pl.ds(2 * at + 1, 256, stride=2), :]], axis=1
                )
                rows = lax.broadcasted_iota(I32, (256, 256), 0) + i * 256
                x = jnp.where(rows < count, x, 0.0)
                high = x.astype(BF16)
                low = (x - high.astype(F32)).astype(BF16)
                sums_ref[...] += dot(high, jnp.concatenate([high, low], axis=1), ((0,), (0,)))
                return _

            lax.fori_loop(0, (count + 255) // 256, add, 0)
            cross = sums_ref[:, 256:]
            gram = (sums_ref[:, :256] + cross + cross.T) * scale
            turned = pltpu.roll(gram, COEFFS, 1)
            ref = slice(0, 64)
            obs = slice(64, 128)
            tim = slice(128, 192)
            put(u, 0, jnp.where(left, gram[ref, 0:128], turned[ref, 128:256]))
            put(u, 128, jnp.where(left, turned[ref, 128:256], turned[tim, 128:256]))
            put(u, 256, jnp.where(left, turned[tim, 128:256], gram[obs, 0:128]))
            return _

        lax.fori_loop(0, UNITS, unit_gram, 0)


def join(plan, times, obs, reply, scale, *old):
    smem = pl.BlockSpec(memory_space=pltpu.SMEM)
    once = functools.partial(pl.BlockSpec, pipeline_mode=pl.Buffered(1))
    return pl.pallas_call(
        functools.partial(join_kernel, scale),
        grid=(JOIN_STEPS,),
        out_shape=jax.ShapeDtypeStruct((UNITS, COEFFS, 384), F32),
        in_specs=[
            smem,
            smem,
            smem,
            once((128, 128), lambda i: (0, 0)),
            pl.BlockSpec((COEFFS, JOIN_BLOCKS * 128), lambda i: (0, i)),
            ANY_SPEC,
        ] + [ANY_SPEC] * len(old),
        out_specs=once((UNITS, COEFFS, 384), lambda i: (0, 0, 0)),
        scratch_shapes=[
            pltpu.VMEM((2 * LINES + 8, 128), F32),
            pltpu.VMEM((2 * DUMP + 8, 128), F32),
            pltpu.VMEM((256, 128), F32),
            pltpu.VMEM((256, 512), F32),
            pltpu.SemaphoreType.DMA,
            pltpu.SemaphoreType.DMA,
        ],
        compiler_params=pltpu.CompilerParams(vmem_limit_bytes=62 << 20),
        name="join",
    )(*plan[1:], times, obs, reply.reshape(LINES, 128), *old)


PANEL = 32
QUAD = UNITS // TM


def square(x):
    high = x.astype(BF16)
    rest = x - high.astype(F32)
    mid = rest.astype(BF16)
    low = (rest - mid.astype(F32)).astype(BF16)
    one = jnp.concatenate([high, high, mid, high, low, mid], axis=0)
    two = jnp.concatenate([high, mid, high, low, high, mid], axis=0)
    return dot(one, two, ((0,), (0,)))


def factor(gram, out_ref, work_ref):
    work_ref[...] = jnp.zeros_like(work_ref)
    work_ref[:, 0:64, 0:192] = gram[:, :, 0:192]
    work_ref[:, 64:128, 64:192] = gram[:, :, 192:320]
    work_ref[:, 128:192, 128:192] = gram[:, :, 320:384]
    row = lax.broadcasted_iota(I32, (PANEL, 256), 0)
    col = lax.broadcasted_iota(I32, (PANEL, 256), 1)
    thin = lax.broadcasted_iota(I32, (PANEL, 1), 0)

    def step(i, _):
        at = pl.multiple_of(i * PANEL, PANEL)
        panels = [pltpu.roll(work_ref[m, pl.ds(at, PANEL), :], 256 - at, 1) for m in range(QUAD)]
        for k in range(0, PANEL - 2, 2):
            for m in range(QUAD):
                panel = panels[m]
                p, q = panel[k : k + 1, :], panel[k + 1 : k + 2, :]
                a, b, c = p[:, k : k + 1], p[:, k + 1 : k + 2], q[:, k + 1 : k + 2]
                inverse = 1.0 / (a * c - b * b)
                u = (c * inverse) * p - (b * inverse) * q
                v = (a * inverse) * q - (b * inverse) * p
                left = jnp.where(thin > k + 1, panel[:, k : k + 1], 0.0)
                right = jnp.where(thin > k + 1, panel[:, k + 1 : k + 2], 0.0)
                panels[m] = panel - left * u - right * v
        for m in range(QUAD):
            panel = panels[m]
            above = pltpu.roll(panel, 1, 0)
            b = jnp.sum(jnp.where(col == row, above, 0.0), axis=1, keepdims=True)
            a = jnp.sum(jnp.where(col == row - 1, above, 0.0), axis=1, keepdims=True)
            second = (thin & 1) == 1
            panel = panel - jnp.where(second, b / jnp.where(second, a, 1.0), 0.0) * above
            diag = jnp.sum(jnp.where(col == row, panel, 0.0), axis=1, keepdims=True)
            panel = jnp.where((col >= row) & (col < 192 - at), panel * (1.0 / jnp.sqrt(diag)), 0.0)
            panel = pltpu.roll(panel, at, 1)
            out_ref[m, pl.ds(at, PANEL), :] = panel[:, :192]
            update = square(panel)
            work_ref[m] = work_ref[m] - update[:192, :]
        return _

    lax.fori_loop(0, 192 // PANEL, step, 0)


def reduce_kernel(gram_ref, out_ref, pair_ref, sum_ref, part_ref, relay_ref, work_ref,
                  pair_send, pair_recv, ring_send, ring_recv):
    sky, tm = lax.axis_index("sky"), lax.axis_index("tm")
    z, core = tm // 2, lax.rem(tm, 2)
    up, down, far = lax.rem(z + 1, 4), lax.rem(z + 3, 4), lax.rem(z + 2, 4)
    partner = (sky, z * 2 + 1 - core)
    above, below = (sky, up * 2 + core), (sky, down * 2 + core)

    barrier = pltpu.get_barrier_semaphore()
    for other in (partner, above, below):
        pl.semaphore_signal(barrier, inc=1, device_id=other, device_id_type=MESH)
    pl.semaphore_wait(barrier, 3)

    pairs = []
    for n, at in enumerate((far, up, down, z)):
        copy = pltpu.make_async_remote_copy(
            src_ref=gram_ref.at[at * 2 + 1 - core], dst_ref=pair_ref.at[at],
            send_sem=pair_send.at[n], recv_sem=pair_recv.at[n], device_id=partner, device_id_type=MESH,
        )
        copy.start()
        pairs.append(copy)

    def join_pair(n, at):
        pairs[n].wait_recv()
        sum_ref[at] = gram_ref[at * 2 + core] + pair_ref[at]

    def ring(n, src, to):
        copy = pltpu.make_async_remote_copy(
            src_ref=src, dst_ref=part_ref.at[n],
            send_sem=ring_send.at[n], recv_sem=ring_recv.at[n], device_id=to, device_id_type=MESH,
        )
        copy.start()
        return copy

    first, second = pl.ds(0, 2), pl.ds(2, 2)
    join_pair(0, far)
    far_up = ring(0, sum_ref.at[far, first], above)
    far_down = ring(1, sum_ref.at[far, second], below)
    join_pair(1, up)
    near_up = ring(2, sum_ref.at[up, second], above)
    join_pair(2, down)
    near_down = ring(3, sum_ref.at[down, first], below)
    far_up.wait_recv()
    relay_ref[0] = part_ref[0] + sum_ref[up, 0:2]
    last_up = ring(4, relay_ref.at[0], above)
    far_down.wait_recv()
    relay_ref[1] = part_ref[1] + sum_ref[down, 2:4]
    last_down = ring(5, relay_ref.at[1], below)
    join_pair(3, z)
    near_down.wait_recv()
    near_up.wait_recv()
    sum_ref[z, 0:2] = sum_ref[z, 0:2] + part_ref[3]
    sum_ref[z, 2:4] = sum_ref[z, 2:4] + part_ref[2]
    last_up.wait_recv()
    last_down.wait_recv()
    total = jnp.concatenate([sum_ref[z, 0:2] + part_ref[4], sum_ref[z, 2:4] + part_ref[5]], axis=0)
    for copy in (*pairs, far_up, far_down, near_up, near_down, last_up, last_down):
        copy.wait_send()
    factor(total, out_ref, work_ref)


def reduce_factor(gram):
    vmem = pl.BlockSpec(memory_space=pltpu.VMEM)
    return pl.pallas_call(
        reduce_kernel,
        out_shape=jax.ShapeDtypeStruct((QUAD, 192, 192), F32),
        in_specs=[vmem],
        out_specs=vmem,
        scratch_shapes=[
            pltpu.VMEM((4, QUAD, COEFFS, 384), F32),
            pltpu.VMEM((4, QUAD, COEFFS, 384), F32),
            pltpu.VMEM((6, 2, COEFFS, 384), F32),
            pltpu.VMEM((2, 2, COEFFS, 384), F32),
            pltpu.VMEM((QUAD, 192, 256), F32),
            pltpu.SemaphoreType.DMA((4,)),
            pltpu.SemaphoreType.DMA((4,)),
            pltpu.SemaphoreType.DMA((6,)),
            pltpu.SemaphoreType.DMA((6,)),
        ],
        compiler_params=pltpu.CompilerParams(collective_id=1, has_side_effects=True),
        name="reduce_factor",
    )(gram.reshape(TM, QUAD, COEFFS, 384))


def per_device(reference_spectra, observed, epoch_time, owner, source_row, unit):
    obs = observed[0].T
    times = epoch_time.reshape(128, 128)
    owners = owner.reshape(128, 128)
    rows = source_row.reshape(128, 128)
    units = unit.reshape(128, 128)
    scale = UNITS / (E_DEV * TM)
    number = jnp.zeros((1,), I32)
    table, *plan = prepare(number, owners, rows, units, reference_spectra.T)

    replies, more = exchange(0, plan[0], table)
    gram = join(plan, times, obs, replies, scale)

    def next_round(state):
        number, _, gram = state
        number = number + 1
        plan = route(number, owners, rows, units)
        replies, more = exchange(3, plan[0], table)
        return number, more, join(plan, times, obs, replies, scale, gram)

    gram = lax.while_loop(lambda state: state[1][0, 0] > 0, next_round, (number, more, gram))[2]
    return reduce_factor(gram)[None]


def solution(mesh):
    placed = (
        P("sky", None),
        P("sky", "tm", None),
        P("sky", "tm"),
        P("sky", "tm", None),
        P("sky", "tm"),
        P("sky", "tm", None),
    )
    return jax.shard_map(
        per_device,
        mesh=mesh,
        in_specs=placed,
        out_specs=P("sky", "tm", None, None),
        check_vma=False,
    )
```

```python
import functools

import jax
import jax.numpy as jnp
from jax import lax
from jax.experimental import pallas as pl
from jax.experimental.pallas import tpu as pltpu
from jax.sharding import PartitionSpec as P

UNITS = 32
COEFFS = 64
SKY = 16
TM = 8
DEVS = SKY * TM
E_DEV = 16384
STRIPE = 512
CLASSES = DEVS // 2
SLOTS = 352
HALF = SLOTS // 2
LINES = CLASSES * HALF
BLOCK = 256
F32 = jnp.float32
BF16 = jnp.bfloat16
I32 = jnp.int32


def dot(a, b, dims, precision=None):
    return lax.dot_general(a, b, (dims, ((), ())), precision=precision, preferred_element_type=F32)


def route_body(round_ref, owner_ref, row_ref, unit_ref, req_ref, epoch_ref, reply_ref, span_ref,
               acc_ref, sort_ref, slot_ref, rank_ref):
    first = round_ref[0] * SLOTS
    tri_row = lax.broadcasted_iota(I32, (BLOCK, BLOCK + 128), 0)
    tri_col = lax.broadcasted_iota(I32, (BLOCK, BLOCK + 128), 1)
    before = ((tri_row < tri_col) | (tri_col >= BLOCK)).astype(BF16)
    classes = lax.broadcasted_iota(I32, (CLASSES, BLOCK), 0)
    units = lax.broadcasted_iota(I32, (UNITS, BLOCK), 0)
    ranks = lax.broadcasted_iota(I32, (SLOTS, BLOCK), 0)
    acc_ref[...] = jnp.zeros_like(acc_ref)

    def pair(ref, b):
        return jnp.concatenate([ref[pl.ds(2 * b, 1), :], ref[pl.ds(2 * b + 1, 1), :]], axis=1)

    def wide(base):
        return jnp.concatenate([base, base], axis=1)

    def step(b, carry):
        base, unit_base = carry
        owner, row, unit = pair(owner_ref, b), pair(row_ref, b), pair(unit_ref, b)
        group = row >> 9
        local = (owner << 9) + (row & (STRIPE - 1))
        hot = classes == group
        ahead = dot(hot.astype(BF16), before, ((1,), (0,)))
        rank = jnp.sum(jnp.where(hot, ahead[:, :BLOCK] + wide(base), 0.0), axis=0, keepdims=True)
        rank = rank.astype(I32) - first
        active = (rank >= 0) & (rank < SLOTS)
        upper = jnp.where(rank >= HALF, 1, 0)
        slot = upper * LINES + group * HALF + rank - upper * HALF
        slot = jnp.where(active, slot, 0)
        high = (local >> 6).astype(F32)
        low = (local & 63).astype(F32)
        values = jnp.concatenate([jnp.where(hot, high, 0.0), jnp.where(hot, low, 0.0)], axis=0).astype(BF16)
        put = (ranks == rank).astype(BF16)
        acc_ref[...] += dot(values, put, ((1,), (1,)))
        mine = (units == unit) & active
        unit_ahead = dot(mine.astype(BF16), before, ((1,), (0,)))
        unit_rank = jnp.sum(jnp.where(mine, unit_ahead[:, :BLOCK] + wide(unit_base), 0.0), axis=0, keepdims=True)
        unit_rank = jnp.where(active, unit_rank.astype(I32), -2 * E_DEV)
        for half in range(2):
            lanes = slice(half * 128, half * 128 + 128)
            slot_ref[pl.ds(2 * b + half, 1), :] = slot[:, lanes]
            rank_ref[pl.ds(2 * b + half, 1), :] = unit_rank[:, lanes]
        return base + ahead[:, BLOCK:], unit_base + unit_ahead[:, BLOCK:]

    start = (jnp.zeros((CLASSES, 128), F32), jnp.zeros((UNITS, 128), F32))
    base, unit_base = lax.fori_loop(0, E_DEV // BLOCK, step, start, unroll=4)
    ends = unit_base
    unit_row = lax.broadcasted_iota(I32, (UNITS, 128), 0)
    for shift in (1, 2, 4, 8, 16):
        ends = ends + jnp.where(unit_row >= shift, pltpu.roll(ends, shift, 0), 0.0)
    begins = ends - unit_base
    span_ref[0:UNITS, :] = unit_base.astype(I32)
    span_ref[UNITS:, :] = begins.astype(I32)
    sort_ref[...] = jnp.zeros_like(sort_ref)
    lines = lax.broadcasted_iota(I32, (128, BLOCK), 0)
    lane = lax.broadcasted_iota(I32, (1, BLOCK), 1)

    def sort(b, _):
        slot, unit_rank, unit = pair(slot_ref, b), pair(rank_ref, b), pair(unit_ref, b)
        begin = jnp.sum(jnp.where(units == unit, wide(begins), 0.0), axis=0, keepdims=True)
        place = unit_rank + begin.astype(I32)
        epoch = b * BLOCK + lane
        hot = lines == (place >> 7)
        pieces = (epoch >> 7, epoch & 127, slot >> 8, slot & 255)
        values = jnp.concatenate([jnp.where(hot, v.astype(F32), 0.0) for v in pieces], axis=0).astype(BF16)
        put = (lines == (place & 127)).astype(BF16)
        sort_ref[...] += dot(values, put, ((1,), (1,)))
        return _

    lax.fori_loop(0, E_DEV // BLOCK, sort, 0, unroll=4)
    epoch_ref[...] = (sort_ref[0:128, :] * 128.0 + sort_ref[128:256, :]).astype(I32)
    reply_ref[...] = (sort_ref[256:384, :] * 256.0 + sort_ref[384:512, :]).astype(I32)
    more = (jnp.max(base).astype(I32) > first + SLOTS).astype(I32)
    wanted = (acc_ref[0:CLASSES, :] * 64.0 + acc_ref[CLASSES:, :]).astype(I32)
    req_ref[:, 0, :] = wanted[:, 0:128]
    req_ref[:, 1, :] = wanted[:, 128:256]
    req_ref[:, 2, :] = jnp.concatenate([wanted[:, 256:], jnp.zeros((CLASSES, 384 - SLOTS), I32)], axis=1)
    req_ref[:, 3, :] = jnp.zeros((CLASSES, 128), I32) + more


PLAN = (
    jax.ShapeDtypeStruct((CLASSES, 4, 128), I32),
    jax.ShapeDtypeStruct((128, 128), I32),
    jax.ShapeDtypeStruct((128, 128), I32),
    jax.ShapeDtypeStruct((2 * UNITS, 128), I32),
)
ROUTE_SCRATCH = [
    pltpu.VMEM((2 * CLASSES, SLOTS), F32),
    pltpu.VMEM((512, 128), F32),
    pltpu.VMEM((128, 128), I32),
    pltpu.VMEM((128, 128), I32),
]
SMEM_SPEC = pl.BlockSpec(memory_space=pltpu.SMEM)
VMEM_SPEC = pl.BlockSpec(memory_space=pltpu.VMEM)
ANY_SPEC = pl.BlockSpec(memory_space=pl.ANY)


def route(number, owner, row, unit):
    return pl.pallas_call(
        route_body,
        out_shape=PLAN,
        in_specs=[SMEM_SPEC, VMEM_SPEC, VMEM_SPEC, VMEM_SPEC],
        out_specs=(VMEM_SPEC,) * 4,
        scratch_shapes=ROUTE_SCRATCH,
        name="route",
    )(number, owner, row, unit)


MESH = pl.DeviceIdType.MESH
def nearer(i):
    x, y, z = i % 4, i // 4 % 4, i // 16
    hops = min(x, 4 - x) + min(y, 4 - y) + z
    if hops != 3:
        return int(hops > 3)
    if z == 0:
        return int(y == 2)
    return int(x != y) if x % 2 and y % 2 else int(x == 2)


FLIPS = sum(nearer(i) << i for i in range(32))


def position():
    sky, tm = lax.axis_index("sky"), lax.axis_index("tm")
    return sky & 3, sky >> 2, tm >> 1, tm & 1


def moved(at, offset):
    x, y, z, core = (a + o for a, o in zip(at, offset))
    return x & 3, y & 3, z & 3, core & 1


def mesh_id(at):
    x, y, z, core = at
    return y * 4 + x, z * 2 + core


def class_of(at):
    x, y, z, core = at
    turned = z & 2
    return ((z & 1) * 2 + core) * 16 + ((y + turned) & 3) * 4 + ((x + turned) & 3)


def turn_of(k):
    step = 13 + 6 * (lax.axis_index("tm") & 1)
    return ((k * step) & 31) + (k & 32)


def near_offset(n):
    i = n & 31
    flip = ((FLIPS >> i) & 1) * 2
    return (i & 3) + flip, (i >> 2) + flip, (i >> 4) + flip, n >> 5


def next_device(k):
    to = lax.axis_index("sky") * TM + lax.axis_index("tm") + k
    return (to >> 3) & (SKY - 1), to & (TM - 1)


def prepare_kernel(round_ref, owner_ref, row_ref, unit_ref, tab_ref,
                   table_ref, req_ref, epoch_ref, reply_ref, span_ref, acc_ref, sort_ref, slot_ref, rank_ref,
                   send_sem, recv_sem):
    here = position()
    x, y, z, core = here
    sky = y * 4 + x

    def other(k):
        return (x + k) & 3, (y + (k >> 2)) & 3, z, core

    def piece(at):
        return tab_ref.at[:, pl.ds(pl.multiple_of(class_of(at) * STRIPE, STRIPE), STRIPE)]

    barrier = pltpu.get_barrier_semaphore()

    def greet(k, _):
        pl.semaphore_signal(barrier, inc=1, device_id=mesh_id(other(k)), device_id_type=MESH)
        return _

    lax.fori_loop(1, SKY, greet, 0)
    pl.semaphore_wait(barrier, SKY - 1)

    def give(k, _):
        at = other((k * 7) & (SKY - 1))
        pltpu.make_async_remote_copy(
            src_ref=piece(at), dst_ref=table_ref.at[sky], send_sem=send_sem, recv_sem=recv_sem,
            device_id=mesh_id(at), device_id_type=MESH,
        ).start()
        return _

    lax.fori_loop(1, SKY, give, 0)
    pltpu.make_async_copy(piece(here), table_ref.at[sky], recv_sem).start()
    route_body(round_ref, owner_ref, row_ref, unit_ref, req_ref, epoch_ref, reply_ref, span_ref,
               acc_ref, sort_ref, slot_ref, rank_ref)
    pltpu.make_async_copy(table_ref.at[pl.ds(0, SKY - 1)], table_ref.at[pl.ds(0, SKY - 1)], send_sem).wait()
    pltpu.make_async_copy(table_ref, table_ref, recv_sem).wait()


def prepare(number, owner, row, unit, spectra):
    return pl.pallas_call(
        prepare_kernel,
        out_shape=(jax.ShapeDtypeStruct((SKY, COEFFS, STRIPE), F32),) + PLAN,
        in_specs=[SMEM_SPEC, VMEM_SPEC, VMEM_SPEC, VMEM_SPEC, ANY_SPEC],
        out_specs=(VMEM_SPEC,) * 5,
        scratch_shapes=ROUTE_SCRATCH + [pltpu.SemaphoreType.DMA] * 2,
        compiler_params=pltpu.CompilerParams(collective_id=2, has_side_effects=True),
        name="prepare",
    )(number, owner, row, unit, spectra)


def exchange_kernel(req_ref, tab_ref, epoch_ref, time_ref, obs_ref, out_ref, more_ref, sorted_ref,
                    rows_ref, asked_ref, flag_ref, index_ref, send_ref, obs_here, local_ref, order_ref,
                    obs_sem, sorted_sem, ask_send, ask_recv, flag_send, flag_recv, local, send_sem, recv_sem):
    here = position()
    mine = class_of(here)
    half_turn = (2, 2, 2, 0)

    barrier = pltpu.get_barrier_semaphore()

    def greet(k, _):
        pl.semaphore_signal(barrier, inc=1, device_id=next_device(k), device_id_type=MESH)
        return _

    lax.fori_loop(1, DEVS, greet, 0)
    pl.semaphore_wait(barrier, DEVS - 1)

    obs_copy = pltpu.make_async_copy(obs_ref, obs_here, obs_sem)
    obs_copy.start()

    def ask(k, _):
        n = turn_of(k)
        at = moved(here, near_offset(n))
        pltpu.make_async_remote_copy(
            src_ref=req_ref.at[class_of(at)], dst_ref=asked_ref.at[n], send_sem=ask_send, recv_sem=ask_recv,
            device_id=mesh_id(at), device_id_type=MESH,
        ).start()
        return _

    def tell(n, _):
        at = moved(moved(here, near_offset(n)), half_turn)
        pltpu.make_async_remote_copy(
            src_ref=req_ref.at[0], dst_ref=flag_ref.at[n], send_sem=flag_send, recv_sem=flag_recv,
            device_id=mesh_id(at), device_id_type=MESH,
        ).start()
        return _

    lax.fori_loop(1, CLASSES, ask, 0)
    pltpu.make_async_copy(req_ref.at[mine], asked_ref.at[0], ask_recv).start()
    lax.fori_loop(0, CLASSES, tell, 0)

    for region in range(SKY):
        block = tab_ref[region]
        rows_ref[region * STRIPE : (region + 1) * STRIPE, :] = jnp.concatenate([block, block], axis=0).T

    pltpu.make_async_copy(asked_ref, asked_ref, ask_recv).wait()
    into = pltpu.make_async_copy(asked_ref, index_ref, local)
    into.start()
    into.wait()

    left = lax.broadcasted_iota(I32, (1, 128), 1) < COEFFS

    def gather(k):
        for j in range(HALF):
            a = index_ref[k, j // 128, j % 128]
            b = index_ref[k, (j + HALF) // 128, (j + HALF) % 128]
            send_ref[k, j : j + 1, :] = jnp.where(left, rows_ref[pl.ds(a, 1), :], rows_ref[pl.ds(b, 1), :])

    def send(k):
        n = turn_of(k)
        pltpu.make_async_remote_copy(
            src_ref=send_ref.at[n], dst_ref=out_ref.at[mine], send_sem=send_sem, recv_sem=recv_sem,
            device_id=mesh_id(moved(here, [-o for o in near_offset(n)])), device_id_type=MESH,
        ).start()

    def serve(k, _):
        gather(turn_of(k))

        @pl.when(k > 1)
        def _():
            send(k - 1)

        return 0

    lax.fori_loop(1, CLASSES, serve, 0)
    gather(0)
    send(CLASSES - 1)
    pltpu.make_async_copy(send_ref.at[0], out_ref.at[mine], recv_sem).start()

    obs_copy.wait()

    def turn(b, _):
        at = pl.multiple_of(b * 128, 128)
        times = jnp.broadcast_to(time_ref[pl.ds(b, 1), :], (COEFFS, 128))
        local_ref[pl.ds(at, 128), :] = jnp.concatenate([times, obs_here[:, pl.ds(at, 128)]], axis=0).T
        return _

    lax.fori_loop(0, 128, turn, 0)

    def put_out(c):
        part = pl.ds(pl.multiple_of(c * SORT_ROWS, SORT_ROWS), SORT_ROWS)
        pltpu.make_async_copy(order_ref.at[part], sorted_ref.at[part], sorted_sem).start()

    def pick(c, _):
        def line(i, _):
            at = pl.multiple_of(c * SORT_ROWS + i * 128, 128)
            for j in range(128):
                e = epoch_ref[c * (SORT_ROWS // 128) + i, j]
                order_ref[pl.ds(at + j, 1), :] = local_ref[pl.ds(e, 1), :]
            return _

        lax.fori_loop(0, SORT_ROWS // 128, line, 0)

        @pl.when(c > 0)
        def _():
            put_out(c - 1)

        return 0

    lax.fori_loop(0, E_DEV // SORT_ROWS, pick, 0)
    put_out(E_DEV // SORT_ROWS - 1)
    most = slice(0, CLASSES - 1)
    pltpu.make_async_copy(asked_ref.at[most], asked_ref.at[most], ask_send).wait()
    pltpu.make_async_copy(flag_ref, flag_ref, flag_send).wait()
    pltpu.make_async_copy(flag_ref, flag_ref, flag_recv).wait()
    more_ref[...] = jnp.maximum(jnp.max(asked_ref[:, 3, :], axis=0, keepdims=True),
                                jnp.max(flag_ref[:, 3, :], axis=0, keepdims=True))
    pltpu.make_async_copy(send_ref.at[most], send_ref.at[most], send_sem).wait()
    pltpu.make_async_copy(sorted_ref, sorted_ref, sorted_sem).wait()
    pltpu.make_async_copy(out_ref, out_ref, recv_sem).wait()


SORT_ROWS = 2048


def exchange(collective, plan, table, times, obs):
    return pl.pallas_call(
        exchange_kernel,
        out_shape=(
            jax.ShapeDtypeStruct((CLASSES, HALF, 128), F32),
            jax.ShapeDtypeStruct((1, 128), I32),
            jax.ShapeDtypeStruct((E_DEV, 128), F32),
        ),
        in_specs=[VMEM_SPEC, VMEM_SPEC, SMEM_SPEC, VMEM_SPEC, ANY_SPEC],
        out_specs=(ANY_SPEC, VMEM_SPEC, ANY_SPEC),
        scratch_shapes=[
            pltpu.VMEM((SKY * STRIPE, 128), F32),
            pltpu.VMEM((CLASSES, 4, 128), I32),
            pltpu.VMEM((CLASSES, 4, 128), I32),
            pltpu.SMEM((CLASSES, 4, 128), I32),
            pltpu.VMEM((CLASSES, HALF, 128), F32),
            pltpu.VMEM((COEFFS, E_DEV), F32),
            pltpu.VMEM((E_DEV, 128), F32),
            pltpu.VMEM((E_DEV, 128), F32),
        ] + [pltpu.SemaphoreType.DMA] * 9,
        compiler_params=pltpu.CompilerParams(collective_id=collective, has_side_effects=True),
        name="exchange",
    )(plan[0], table, plan[1], times, obs)


def join_kernel(scale, line_ref, span_ref, reply_ref, sorted_ref, *refs):
    *old_ref, out_ref, rows_ref, picked_ref, local_ref, sums_ref, sem, local_sem, old_sem = refs
    copy = pltpu.make_async_copy(reply_ref, rows_ref.at[pl.ds(0, LINES), :], sem)
    copy.start()
    local_copy = pltpu.make_async_copy(sorted_ref, local_ref.at[pl.ds(0, E_DEV), :], local_sem)
    local_copy.start()
    for old in old_ref:
        before = pltpu.make_async_copy(old, out_ref, old_sem)
        before.start()
        before.wait()
    copy.wait()

    def turn(i, _):
        at = pl.multiple_of(i * 256, 256)
        rows_ref[pl.ds(LINES + at, 256), :] = pltpu.roll(rows_ref[pl.ds(at, 256), :], COEFFS, 1)
        return _

    lax.fori_loop(0, LINES // 256, turn, 0)

    def pick(c, _):
        at = pl.multiple_of(c * 128, 128)
        for j in range(128):
            picked_ref[pl.ds(at + j, 1), :] = rows_ref[pl.ds(line_ref[c, j], 1), :]
        return _

    lax.fori_loop(0, E_DEV // 128, pick, 0)
    local_copy.wait()
    left = lax.broadcasted_iota(I32, (1, 128), 1) < COEFFS

    def put(u, at, value):
        lanes = slice(at, at + 128)
        out_ref[u, :, lanes] = out_ref[u, :, lanes] + value if old_ref else value

    def unit_gram(u, _):
        count = span_ref[u, 0]
        begin = span_ref[UNITS + u, 0]
        sums_ref[...] = jnp.zeros_like(sums_ref)

        def add(i, _):
            part = pl.ds(begin + i * 256, 256)
            ref, own = picked_ref[part, :], local_ref[part, :]
            x = jnp.concatenate([jnp.where(left, ref, own), ref * own], axis=1)
            rows = lax.broadcasted_iota(I32, (256, 256), 0) + i * 256
            x = jnp.where(rows < count, x, 0.0)
            high = x.astype(BF16)
            low = (x - high.astype(F32)).astype(BF16)
            sums_ref[...] += dot(high, jnp.concatenate([high, low], axis=1), ((0,), (0,)))
            return _

        lax.fori_loop(0, (count + 255) // 256, add, 0)
        cross = sums_ref[:, 256:]
        gram = (sums_ref[:, :256] + cross + cross.T) * scale
        turned = pltpu.roll(gram, COEFFS, 1)
        ref = slice(0, 64)
        obs = slice(64, 128)
        tim = slice(128, 192)
        put(u, 0, jnp.where(left, gram[ref, 0:128], turned[ref, 128:256]))
        put(u, 128, jnp.where(left, turned[ref, 128:256], turned[tim, 128:256]))
        put(u, 256, jnp.where(left, turned[tim, 128:256], gram[obs, 0:128]))
        return _

    lax.fori_loop(0, UNITS, unit_gram, 0)


def join(plan, replies, local, scale, *old):
    return pl.pallas_call(
        functools.partial(join_kernel, scale),
        out_shape=jax.ShapeDtypeStruct((UNITS, COEFFS, 384), F32),
        in_specs=[SMEM_SPEC, SMEM_SPEC, ANY_SPEC, ANY_SPEC] + [ANY_SPEC] * len(old),
        out_specs=VMEM_SPEC,
        scratch_shapes=[
            pltpu.VMEM((2 * LINES, 128), F32),
            pltpu.VMEM((E_DEV + 256, 128), F32),
            pltpu.VMEM((E_DEV + 256, 128), F32),
            pltpu.VMEM((256, 512), F32),
        ] + [pltpu.SemaphoreType.DMA] * 3,
        name="join",
    )(plan[2], plan[3], replies.reshape(LINES, 128), local, *old)


PANEL = 32
QUAD = UNITS // TM


def square(x):
    high = x.astype(BF16)
    rest = x - high.astype(F32)
    mid = rest.astype(BF16)
    low = (rest - mid.astype(F32)).astype(BF16)
    one = jnp.concatenate([high, high, mid, high, low, mid], axis=0)
    two = jnp.concatenate([high, mid, high, low, high, mid], axis=0)
    return dot(one, two, ((0,), (0,)))


def factor(gram, out_ref, work_ref):
    work_ref[...] = jnp.zeros_like(work_ref)
    work_ref[:, 0:64, 0:192] = gram[:, :, 0:192]
    work_ref[:, 64:128, 64:192] = gram[:, :, 192:320]
    work_ref[:, 128:192, 128:192] = gram[:, :, 320:384]
    row = lax.broadcasted_iota(I32, (PANEL, 256), 0)
    col = lax.broadcasted_iota(I32, (PANEL, 256), 1)
    thin = lax.broadcasted_iota(I32, (PANEL, 1), 0)

    def step(i, _):
        at = pl.multiple_of(i * PANEL, PANEL)
        panels = [pltpu.roll(work_ref[m, pl.ds(at, PANEL), :], 256 - at, 1) for m in range(QUAD)]
        for k in range(PANEL - 1):
            for m in range(QUAD):
                panel = panels[m]
                pivot = 1.0 / panel[k : k + 1, k : k + 1]
                below = jnp.where(thin > k, panel[:, k : k + 1] * pivot, 0.0)
                panels[m] = panel - below * panel[k : k + 1, :]
        for m in range(QUAD):
            panel = panels[m]
            diag = jnp.sum(jnp.where(col == row, panel, 0.0), axis=1, keepdims=True)
            panel = jnp.where((col >= row) & (col < 192 - at), panel * (1.0 / jnp.sqrt(diag)), 0.0)
            panel = pltpu.roll(panel, at, 1)
            out_ref[m, pl.ds(at, PANEL), :] = panel[:, :192]
            update = square(panel)
            work_ref[m] = work_ref[m] - update[:192, :]
        return _

    lax.fori_loop(0, 192 // PANEL, step, 0)


def reduce_kernel(gram_ref, out_ref, pair_ref, sum_ref, part_ref, relay_ref, work_ref,
                  pair_send, pair_recv, ring_send, ring_recv):
    sky, tm = lax.axis_index("sky"), lax.axis_index("tm")
    z, core = tm // 2, lax.rem(tm, 2)
    up, down, far = lax.rem(z + 1, 4), lax.rem(z + 3, 4), lax.rem(z + 2, 4)
    partner = (sky, z * 2 + 1 - core)
    above, below = (sky, up * 2 + core), (sky, down * 2 + core)

    barrier = pltpu.get_barrier_semaphore()
    for other in (partner, above, below):
        pl.semaphore_signal(barrier, inc=1, device_id=other, device_id_type=MESH)
    pl.semaphore_wait(barrier, 3)

    pairs = []
    for n, at in enumerate((far, up, down, z)):
        copy = pltpu.make_async_remote_copy(
            src_ref=gram_ref.at[at * 2 + 1 - core], dst_ref=pair_ref.at[at],
            send_sem=pair_send.at[n], recv_sem=pair_recv.at[n], device_id=partner, device_id_type=MESH,
        )
        copy.start()
        pairs.append(copy)

    def join_pair(n, at):
        pairs[n].wait_recv()
        sum_ref[at] = gram_ref[at * 2 + core] + pair_ref[at]

    def ring(n, src, to):
        copy = pltpu.make_async_remote_copy(
            src_ref=src, dst_ref=part_ref.at[n],
            send_sem=ring_send.at[n], recv_sem=ring_recv.at[n], device_id=to, device_id_type=MESH,
        )
        copy.start()
        return copy

    first, second = pl.ds(0, 2), pl.ds(2, 2)
    join_pair(0, far)
    far_up = ring(0, sum_ref.at[far, first], above)
    far_down = ring(1, sum_ref.at[far, second], below)
    join_pair(1, up)
    near_up = ring(2, sum_ref.at[up, second], above)
    join_pair(2, down)
    near_down = ring(3, sum_ref.at[down, first], below)
    far_up.wait_recv()
    relay_ref[0] = part_ref[0] + sum_ref[up, 0:2]
    last_up = ring(4, relay_ref.at[0], above)
    far_down.wait_recv()
    relay_ref[1] = part_ref[1] + sum_ref[down, 2:4]
    last_down = ring(5, relay_ref.at[1], below)
    join_pair(3, z)
    near_down.wait_recv()
    near_up.wait_recv()
    sum_ref[z, 0:2] = sum_ref[z, 0:2] + part_ref[3]
    sum_ref[z, 2:4] = sum_ref[z, 2:4] + part_ref[2]
    last_up.wait_recv()
    last_down.wait_recv()
    total = jnp.concatenate([sum_ref[z, 0:2] + part_ref[4], sum_ref[z, 2:4] + part_ref[5]], axis=0)
    for copy in (*pairs, far_up, far_down, near_up, near_down, last_up, last_down):
        copy.wait_send()
    factor(total, out_ref, work_ref)


def reduce_factor(gram):
    vmem = pl.BlockSpec(memory_space=pltpu.VMEM)
    return pl.pallas_call(
        reduce_kernel,
        out_shape=jax.ShapeDtypeStruct((QUAD, 192, 192), F32),
        in_specs=[vmem],
        out_specs=vmem,
        scratch_shapes=[
            pltpu.VMEM((4, QUAD, COEFFS, 384), F32),
            pltpu.VMEM((4, QUAD, COEFFS, 384), F32),
            pltpu.VMEM((6, 2, COEFFS, 384), F32),
            pltpu.VMEM((2, 2, COEFFS, 384), F32),
            pltpu.VMEM((QUAD, 192, 256), F32),
            pltpu.SemaphoreType.DMA((4,)),
            pltpu.SemaphoreType.DMA((4,)),
            pltpu.SemaphoreType.DMA((6,)),
            pltpu.SemaphoreType.DMA((6,)),
        ],
        compiler_params=pltpu.CompilerParams(collective_id=1, has_side_effects=True),
        name="reduce_factor",
    )(gram.reshape(TM, QUAD, COEFFS, 384))


def per_device(reference_spectra, observed, epoch_time, owner, source_row, unit):
    obs = observed[0].T
    times = epoch_time.reshape(128, 128)
    owners = owner.reshape(128, 128)
    rows = source_row.reshape(128, 128)
    units = unit.reshape(128, 128)
    scale = UNITS / (E_DEV * TM)
    number = jnp.zeros((1,), I32)
    table, *plan = prepare(number, owners, rows, units, reference_spectra.T)

    replies, more, local = exchange(0, plan, table, times, obs)
    gram = join(plan, replies, local, scale)

    def next_round(state):
        number, _, gram = state
        number = number + 1
        plan = route(number, owners, rows, units)
        replies, more, local = exchange(3, plan, table, times, obs)
        return number, more, join(plan, replies, local, scale, gram)

    gram = lax.while_loop(lambda state: state[1][0, 0] > 0, next_round, (number, more, gram))[2]
    return reduce_factor(gram)[None]


def solution(mesh):
    placed = (
        P("sky", None),
        P("sky", "tm", None),
        P("sky", "tm"),
        P("sky", "tm", None),
        P("sky", "tm"),
        P("sky", "tm", None),
    )
    return jax.shard_map(
        per_device,
        mesh=mesh,
        in_specs=placed,
        out_specs=P("sky", "tm", None, None),
        check_vma=False,
    )
```

```python
import functools

import jax
import jax.numpy as jnp
from jax import lax
from jax.experimental import pallas as pl
from jax.experimental.pallas import tpu as pltpu
from jax.sharding import PartitionSpec as P

UNITS = 32
COEFFS = 64
SKY = 16
TM = 8
DEVS = SKY * TM
E_DEV = 16384
STRIPE = 512
CLASSES = DEVS // 2
SLOTS = 352
HALF = SLOTS // 2
LINES = CLASSES * HALF
BLOCK = 256
F32 = jnp.float32
BF16 = jnp.bfloat16
I32 = jnp.int32


def dot(a, b, dims, precision=None):
    return lax.dot_general(a, b, (dims, ((), ())), precision=precision, preferred_element_type=F32)


def exact(small):
    return small.astype(F32).astype(BF16)


def route_body(round_ref, owner_ref, row_ref, unit_ref, req_ref, epoch_ref, reply_ref, span_ref,
               acc_ref, sort_ref, slot_ref, rank_ref):
    first = round_ref[0] * SLOTS
    tri_row = lax.broadcasted_iota(I32, (BLOCK, BLOCK + 128), 0)
    tri_col = lax.broadcasted_iota(I32, (BLOCK, BLOCK + 128), 1)
    before = ((tri_row < tri_col) | (tri_col >= BLOCK)).astype(BF16)
    classes = lax.broadcasted_iota(I32, (CLASSES, BLOCK), 0)
    units = lax.broadcasted_iota(I32, (UNITS, BLOCK), 0)
    ranks = lax.broadcasted_iota(I32, (SLOTS, BLOCK), 0)
    acc_ref[...] = jnp.zeros_like(acc_ref)

    def pair(ref, b):
        return jnp.concatenate([ref[pl.ds(2 * b, 1), :], ref[pl.ds(2 * b + 1, 1), :]], axis=1)

    def wide(base):
        return jnp.concatenate([base, base], axis=1)

    def step(b, carry):
        base, unit_base = carry
        owner, row, unit = pair(owner_ref, b), pair(row_ref, b), pair(unit_ref, b)
        group = row >> 9
        local = (owner << 9) + (row & (STRIPE - 1))
        hot = classes == group
        hot_one = hot.astype(BF16)
        ahead = dot(hot_one, before, ((1,), (0,)))
        rank = jnp.sum(jnp.where(hot, ahead[:, :BLOCK] + wide(base), 0.0), axis=0, keepdims=True)
        rank = rank.astype(I32) - first
        active = (rank >= 0) & (rank < SLOTS)
        upper = jnp.where(rank >= HALF, 1, 0)
        slot = upper * LINES + group * HALF + rank - upper * HALF
        slot = jnp.where(active, slot, 0)
        values = jnp.concatenate([hot_one * exact(local >> 6), hot_one * exact(local & 63)], axis=0)
        put = (ranks == rank).astype(BF16)
        acc_ref[...] += dot(values, put, ((1,), (1,)))
        mine = (units == unit) & active
        unit_ahead = dot(mine.astype(BF16), before, ((1,), (0,)))
        unit_rank = jnp.sum(jnp.where(mine, unit_ahead[:, :BLOCK] + wide(unit_base), 0.0), axis=0, keepdims=True)
        unit_rank = jnp.where(active, unit_rank.astype(I32), -2 * E_DEV)
        for half in range(2):
            lanes = slice(half * 128, half * 128 + 128)
            slot_ref[pl.ds(2 * b + half, 1), :] = slot[:, lanes]
            rank_ref[pl.ds(2 * b + half, 1), :] = unit_rank[:, lanes]
        return base + ahead[:, BLOCK:], unit_base + unit_ahead[:, BLOCK:]

    start = (jnp.zeros((CLASSES, 128), F32), jnp.zeros((UNITS, 128), F32))
    base, unit_base = lax.fori_loop(0, E_DEV // BLOCK, step, start, unroll=4)
    ends = unit_base
    unit_row = lax.broadcasted_iota(I32, (UNITS, 128), 0)
    for shift in (1, 2, 4, 8, 16):
        ends = ends + jnp.where(unit_row >= shift, pltpu.roll(ends, shift, 0), 0.0)
    begins = ends - unit_base
    span_ref[0:UNITS, :] = unit_base.astype(I32)
    span_ref[UNITS:, :] = begins.astype(I32)
    sort_ref[...] = jnp.zeros_like(sort_ref)
    lines = lax.broadcasted_iota(I32, (128, BLOCK), 0)
    lane = lax.broadcasted_iota(I32, (1, BLOCK), 1)

    def sort(b, _):
        slot, unit_rank, unit = pair(slot_ref, b), pair(rank_ref, b), pair(unit_ref, b)
        begin = jnp.sum(jnp.where(units == unit, wide(begins), 0.0), axis=0, keepdims=True)
        place = unit_rank + begin.astype(I32)
        epoch = b * BLOCK + lane
        hot_one = (lines == (place >> 7)).astype(BF16)
        pieces = (epoch >> 7, epoch & 127, slot >> 8, slot & 255)
        values = jnp.concatenate([hot_one * exact(v) for v in pieces], axis=0)
        put = (lines == (place & 127)).astype(BF16)
        sort_ref[...] += dot(values, put, ((1,), (1,)))
        return _

    lax.fori_loop(0, E_DEV // BLOCK, sort, 0, unroll=4)
    epoch_ref[...] = (sort_ref[0:128, :] * 128.0 + sort_ref[128:256, :]).astype(I32)
    reply_ref[...] = (sort_ref[256:384, :] * 256.0 + sort_ref[384:512, :]).astype(I32)
    more = (jnp.max(base).astype(I32) > first + SLOTS).astype(I32)
    wanted = (acc_ref[0:CLASSES, :] * 64.0 + acc_ref[CLASSES:, :]).astype(I32)
    req_ref[:, 0, :] = wanted[:, 0:128]
    req_ref[:, 1, :] = wanted[:, 128:256]
    req_ref[:, 2, :] = jnp.concatenate([wanted[:, 256:], jnp.zeros((CLASSES, 384 - SLOTS), I32)], axis=1)
    req_ref[:, 3, :] = jnp.zeros((CLASSES, 128), I32) + more


PLAN = (
    jax.ShapeDtypeStruct((CLASSES, 4, 128), I32),
    jax.ShapeDtypeStruct((128, 128), I32),
    jax.ShapeDtypeStruct((128, 128), I32),
    jax.ShapeDtypeStruct((2 * UNITS, 128), I32),
)
ROUTE_SCRATCH = [
    pltpu.VMEM((2 * CLASSES, SLOTS), F32),
    pltpu.VMEM((512, 128), F32),
    pltpu.VMEM((128, 128), I32),
    pltpu.VMEM((128, 128), I32),
]
SMEM_SPEC = pl.BlockSpec(memory_space=pltpu.SMEM)
VMEM_SPEC = pl.BlockSpec(memory_space=pltpu.VMEM)
ANY_SPEC = pl.BlockSpec(memory_space=pl.ANY)


def route(number, owner, row, unit):
    return pl.pallas_call(
        route_body,
        out_shape=PLAN,
        in_specs=[SMEM_SPEC, VMEM_SPEC, VMEM_SPEC, VMEM_SPEC],
        out_specs=(VMEM_SPEC,) * 4,
        scratch_shapes=ROUTE_SCRATCH,
        name="route",
    )(number, owner, row, unit)


MESH = pl.DeviceIdType.MESH
def nearer(i):
    x, y, z = i % 4, i // 4 % 4, i // 16
    hops = min(x, 4 - x) + min(y, 4 - y) + z
    if hops != 3:
        return int(hops > 3)
    if z == 0:
        return int(y == 2)
    return int(x != y) if x % 2 and y % 2 else int(x == 2)


FLIPS = sum(nearer(i) << i for i in range(32))


def position():
    sky, tm = lax.axis_index("sky"), lax.axis_index("tm")
    return sky & 3, sky >> 2, tm >> 1, tm & 1


def moved(at, offset):
    x, y, z, core = (a + o for a, o in zip(at, offset))
    return x & 3, y & 3, z & 3, core & 1


def mesh_id(at):
    x, y, z, core = at
    return y * 4 + x, z * 2 + core


def class_of(at):
    x, y, z, core = at
    turned = z & 2
    return ((z & 1) * 2 + core) * 16 + ((y + turned) & 3) * 4 + ((x + turned) & 3)


def turn_of(k):
    step = 13 + 6 * (lax.axis_index("tm") & 1)
    return ((k * step) & 31) + (k & 32)


def near_offset(n):
    i = n & 31
    flip = ((FLIPS >> i) & 1) * 2
    return (i & 3) + flip, (i >> 2) + flip, (i >> 4) + flip, n >> 5


def next_device(k):
    to = lax.axis_index("sky") * TM + lax.axis_index("tm") + k
    return (to >> 3) & (SKY - 1), to & (TM - 1)


def prepare_kernel(round_ref, owner_ref, row_ref, unit_ref, tab_ref,
                   table_ref, req_ref, epoch_ref, reply_ref, span_ref, acc_ref, sort_ref, slot_ref, rank_ref,
                   send_sem, recv_sem):
    here = position()
    x, y, z, core = here
    sky = y * 4 + x

    def other(k):
        return (x + k) & 3, (y + (k >> 2)) & 3, z, core

    def piece(at):
        return tab_ref.at[:, pl.ds(pl.multiple_of(class_of(at) * STRIPE, STRIPE), STRIPE)]

    barrier = pltpu.get_barrier_semaphore()

    def greet(k, _):
        pl.semaphore_signal(barrier, inc=1, device_id=mesh_id(other(k)), device_id_type=MESH)
        return _

    lax.fori_loop(1, SKY, greet, 0)
    pl.semaphore_wait(barrier, SKY - 1)

    def give(k, _):
        at = other((k * 7) & (SKY - 1))
        pltpu.make_async_remote_copy(
            src_ref=piece(at), dst_ref=table_ref.at[sky], send_sem=send_sem, recv_sem=recv_sem,
            device_id=mesh_id(at), device_id_type=MESH,
        ).start()
        return _

    lax.fori_loop(1, SKY, give, 0)
    pltpu.make_async_copy(piece(here), table_ref.at[sky], recv_sem).start()
    route_body(round_ref, owner_ref, row_ref, unit_ref, req_ref, epoch_ref, reply_ref, span_ref,
               acc_ref, sort_ref, slot_ref, rank_ref)
    pltpu.make_async_copy(table_ref.at[pl.ds(0, SKY - 1)], table_ref.at[pl.ds(0, SKY - 1)], send_sem).wait()
    pltpu.make_async_copy(table_ref, table_ref, recv_sem).wait()


def prepare(number, owner, row, unit, spectra):
    return pl.pallas_call(
        prepare_kernel,
        out_shape=(jax.ShapeDtypeStruct((SKY, COEFFS, STRIPE), F32),) + PLAN,
        in_specs=[SMEM_SPEC, VMEM_SPEC, VMEM_SPEC, VMEM_SPEC, ANY_SPEC],
        out_specs=(VMEM_SPEC,) * 5,
        scratch_shapes=ROUTE_SCRATCH + [pltpu.SemaphoreType.DMA] * 2,
        compiler_params=pltpu.CompilerParams(collective_id=2, has_side_effects=True),
        name="prepare",
    )(number, owner, row, unit, spectra)


def exchange_kernel(req_ref, tab_ref, epoch_ref, time_ref, obs_ref, out_ref, more_ref, sorted_ref,
                    rows_ref, asked_ref, flag_ref, index_ref, send_ref, obs_here, local_ref, order_ref,
                    obs_sem, sorted_sem, ask_send, ask_recv, flag_send, flag_recv, local, send_sem, recv_sem):
    here = position()
    mine = class_of(here)
    half_turn = (2, 2, 2, 0)

    barrier = pltpu.get_barrier_semaphore()

    def greet(k, _):
        pl.semaphore_signal(barrier, inc=1, device_id=next_device(k), device_id_type=MESH)
        return _

    lax.fori_loop(1, DEVS, greet, 0)
    pl.semaphore_wait(barrier, DEVS - 1)

    obs_copy = pltpu.make_async_copy(obs_ref, obs_here, obs_sem)
    obs_copy.start()

    def ask(k, _):
        n = turn_of(k)
        at = moved(here, near_offset(n))
        pltpu.make_async_remote_copy(
            src_ref=req_ref.at[class_of(at)], dst_ref=asked_ref.at[n], send_sem=ask_send, recv_sem=ask_recv,
            device_id=mesh_id(at), device_id_type=MESH,
        ).start()
        return _

    def tell(n, _):
        at = moved(moved(here, near_offset(n)), half_turn)
        pltpu.make_async_remote_copy(
            src_ref=req_ref.at[0], dst_ref=flag_ref.at[n], send_sem=flag_send, recv_sem=flag_recv,
            device_id=mesh_id(at), device_id_type=MESH,
        ).start()
        return _

    lax.fori_loop(1, CLASSES, ask, 0)
    pltpu.make_async_copy(req_ref.at[mine], asked_ref.at[0], ask_recv).start()
    lax.fori_loop(0, CLASSES, tell, 0)

    for region in range(SKY):
        block = tab_ref[region]
        rows_ref[region * STRIPE : (region + 1) * STRIPE, :] = jnp.concatenate([block, block], axis=0).T

    pltpu.make_async_copy(asked_ref, asked_ref, ask_recv).wait()
    into = pltpu.make_async_copy(asked_ref, index_ref, local)
    into.start()
    into.wait()

    left = lax.broadcasted_iota(I32, (1, 128), 1) < COEFFS

    def gather(k):
        for j in range(HALF):
            a = index_ref[k, j // 128, j % 128]
            b = index_ref[k, (j + HALF) // 128, (j + HALF) % 128]
            send_ref[k, j : j + 1, :] = jnp.where(left, rows_ref[pl.ds(a, 1), :], rows_ref[pl.ds(b, 1), :])

    def send(k):
        n = turn_of(k)
        pltpu.make_async_remote_copy(
            src_ref=send_ref.at[n], dst_ref=out_ref.at[mine], send_sem=send_sem, recv_sem=recv_sem,
            device_id=mesh_id(moved(here, [-o for o in near_offset(n)])), device_id_type=MESH,
        ).start()

    def serve(k, _):
        gather(turn_of(k))

        @pl.when(k > 1)
        def _():
            send(k - 1)

        return 0

    lax.fori_loop(1, CLASSES, serve, 0)
    gather(0)
    send(CLASSES - 1)
    pltpu.make_async_copy(send_ref.at[0], out_ref.at[mine], recv_sem).start()

    obs_copy.wait()

    def turn(b, _):
        at = pl.multiple_of(b * 128, 128)
        times = jnp.broadcast_to(time_ref[pl.ds(b, 1), :], (COEFFS, 128))
        local_ref[pl.ds(at, 128), :] = jnp.concatenate([times, obs_here[:, pl.ds(at, 128)]], axis=0).T
        return _

    lax.fori_loop(0, 128, turn, 0)

    def put_out(c):
        part = pl.ds(pl.multiple_of(c * SORT_ROWS, SORT_ROWS), SORT_ROWS)
        pltpu.make_async_copy(order_ref.at[part], sorted_ref.at[part], sorted_sem).start()

    def pick(c, _):
        def line(i, _):
            at = pl.multiple_of(c * SORT_ROWS + i * 128, 128)
            for j in range(128):
                e = epoch_ref[c * (SORT_ROWS // 128) + i, j]
                order_ref[pl.ds(at + j, 1), :] = local_ref[pl.ds(e, 1), :]
            return _

        lax.fori_loop(0, SORT_ROWS // 128, line, 0)

        @pl.when(c > 0)
        def _():
            put_out(c - 1)

        return 0

    lax.fori_loop(0, E_DEV // SORT_ROWS, pick, 0)
    put_out(E_DEV // SORT_ROWS - 1)
    most = slice(0, CLASSES - 1)
    pltpu.make_async_copy(asked_ref.at[most], asked_ref.at[most], ask_send).wait()
    pltpu.make_async_copy(flag_ref, flag_ref, flag_send).wait()
    pltpu.make_async_copy(flag_ref, flag_ref, flag_recv).wait()
    more_ref[...] = jnp.maximum(jnp.max(asked_ref[:, 3, :], axis=0, keepdims=True),
                                jnp.max(flag_ref[:, 3, :], axis=0, keepdims=True))
    pltpu.make_async_copy(send_ref.at[most], send_ref.at[most], send_sem).wait()
    pltpu.make_async_copy(sorted_ref, sorted_ref, sorted_sem).wait()
    pltpu.make_async_copy(out_ref, out_ref, recv_sem).wait()


SORT_ROWS = 2048


def exchange(collective, plan, table, times, obs):
    return pl.pallas_call(
        exchange_kernel,
        out_shape=(
            jax.ShapeDtypeStruct((CLASSES, HALF, 128), F32),
            jax.ShapeDtypeStruct((1, 128), I32),
            jax.ShapeDtypeStruct((E_DEV, 128), F32),
        ),
        in_specs=[VMEM_SPEC, VMEM_SPEC, SMEM_SPEC, VMEM_SPEC, ANY_SPEC],
        out_specs=(ANY_SPEC, VMEM_SPEC, ANY_SPEC),
        scratch_shapes=[
            pltpu.VMEM((SKY * STRIPE, 128), F32),
            pltpu.VMEM((CLASSES, 4, 128), I32),
            pltpu.VMEM((CLASSES, 4, 128), I32),
            pltpu.SMEM((CLASSES, 4, 128), I32),
            pltpu.VMEM((CLASSES, HALF, 128), F32),
            pltpu.VMEM((COEFFS, E_DEV), F32),
            pltpu.VMEM((E_DEV, 128), F32),
            pltpu.VMEM((E_DEV, 128), F32),
        ] + [pltpu.SemaphoreType.DMA] * 9,
        compiler_params=pltpu.CompilerParams(collective_id=collective, has_side_effects=True),
        name="exchange",
    )(plan[0], table, plan[1], times, obs)


def join_kernel(scale, line_ref, span_ref, reply_ref, sorted_ref, *refs):
    *old_ref, out_ref, rows_ref, picked_ref, local_ref, sums_ref, sem, local_sem, old_sem = refs
    copy = pltpu.make_async_copy(reply_ref, rows_ref.at[pl.ds(0, LINES), :], sem)
    copy.start()
    local_copy = pltpu.make_async_copy(sorted_ref, local_ref.at[pl.ds(0, E_DEV), :], local_sem)
    local_copy.start()
    for old in old_ref:
        before = pltpu.make_async_copy(old, out_ref, old_sem)
        before.start()
        before.wait()
    copy.wait()

    def turn(i, _):
        at = pl.multiple_of(i * 256, 256)
        rows_ref[pl.ds(LINES + at, 256), :] = pltpu.roll(rows_ref[pl.ds(at, 256), :], COEFFS, 1)
        return _

    lax.fori_loop(0, LINES // 256, turn, 0)

    def pick(c):
        at = pl.multiple_of(c * 256, 256)
        for j in range(256):
            picked_ref[pl.ds(at + j, 1), :] = rows_ref[pl.ds(line_ref[c * 2 + j // 128, j % 128], 1), :]

    pick(0)
    pick(1)
    local_copy.wait()
    left = lax.broadcasted_iota(I32, (1, 128), 1) < COEFFS

    def put(u, at, value):
        lanes = slice(at, at + 128)
        out_ref[u, :, lanes] = out_ref[u, :, lanes] + value if old_ref else value

    def unit_gram(u, done):
        count = span_ref[u, 0]
        begin = span_ref[UNITS + u, 0]
        sums_ref[...] = jnp.zeros_like(sums_ref)

        def add(i, to_pick):
            part = pl.ds(begin + i * 256, 256)
            ref, own = picked_ref[part, :], local_ref[part, :]
            alive = lax.broadcasted_iota(I32, (256, 128), 0) + i * 256 < count
            plain = jnp.where(alive, jnp.where(left, ref, own), 0.0)
            timed = jnp.where(alive & left, ref * own, 0.0)
            plain_high, timed_high = plain.astype(BF16), timed.astype(BF16)
            plain_low = (plain - plain_high.astype(F32)).astype(BF16)
            timed_both = timed_high.astype(F32) + pltpu.roll(timed - timed_high.astype(F32), COEFFS, 1)
            high = jnp.concatenate([plain_high, timed_high], axis=1)[:, :192]
            both = jnp.concatenate([plain_high, plain_low, timed_both.astype(BF16)], axis=1)
            if to_pick is not None:
                pick(to_pick)
            sums_ref[...] += dot(high, both, ((0,), (0,)))

        def add_block(i, done):
            pl.when(done + 2 < E_DEV // 256)(lambda: add(i, done + 2))
            pl.when(done + 2 >= E_DEV // 256)(lambda: add(i, None))
            return done + 1

        done = lax.fori_loop(0, (count + 255) >> 8, add_block, done)
        sums = sums_ref[...] * scale
        near, cross, late = sums[:, 0:128], sums[:, 128:256], sums[:, 256:384]
        cross_t, late_t = cross.T, late.T
        corner = near[0:128] + cross[0:128] + cross_t[:, 0:128]
        late_sum = late[:, 0:64] + late[:, 64:128]
        ref_tim = late_sum[0:64] + cross_t[0:64, 128:192]
        tim_tim = late_sum[128:192] + late_t[64:128, 128:192]
        tim_obs = near[128:192, 64:128] + cross[128:192, 64:128] + late_t[64:128, 64:128]
        put(u, 0, jnp.concatenate([corner[0:64, 0:64], ref_tim], axis=1))
        put(u, 128, jnp.concatenate([corner[0:64, 64:128], tim_tim], axis=1))
        put(u, 256, jnp.concatenate([tim_obs, corner[64:128, 64:128]], axis=1))
        return done

    lax.fori_loop(0, UNITS, unit_gram, 0)


def join(plan, replies, local, scale, *old):
    return pl.pallas_call(
        functools.partial(join_kernel, scale),
        out_shape=jax.ShapeDtypeStruct((UNITS, COEFFS, 384), F32),
        in_specs=[SMEM_SPEC, SMEM_SPEC, ANY_SPEC, ANY_SPEC] + [ANY_SPEC] * len(old),
        out_specs=VMEM_SPEC,
        scratch_shapes=[
            pltpu.VMEM((2 * LINES, 128), F32),
            pltpu.VMEM((E_DEV + 256, 128), F32),
            pltpu.VMEM((E_DEV + 256, 128), F32),
            pltpu.VMEM((192, 384), F32),
        ] + [pltpu.SemaphoreType.DMA] * 3,
        name="join",
    )(plan[2], plan[3], replies.reshape(LINES, 128), local, *old)


PANEL = 16
QUAD = UNITS // TM


def square(x):
    high = x.astype(BF16)
    rest = x - high.astype(F32)
    mid = rest.astype(BF16)
    low = (rest - mid.astype(F32)).astype(BF16)
    one = jnp.concatenate([high, high, mid, high, low, mid], axis=0)
    two = jnp.concatenate([high, mid, high, low, high, mid], axis=0)
    return dot(one, two, ((0,), (0,)))


def factor(gram, out_ref, work_ref, panel_ref):
    def rows_of(m, first, many):
        return pl.ds(first * QUAD + m, many, stride=QUAD)

    def zeros(rows, lanes):
        return jnp.zeros((rows, lanes), F32)

    for m in range(QUAD):
        for n, (lo, hi) in enumerate(((0, 192), (192, 320), (320, 384))):
            parts = [gram[m, :, lo:hi], zeros(64, 64)]
            block = jnp.concatenate([zeros(64, 64 * n)] * (n > 0) + parts, axis=1)
            for tile in range(2):
                work_ref[tile, rows_of(m, 64 * n, 64), :] = block[:, tile * 128 : tile * 128 + 128]

    for start in range(0, 192, PANEL):
        tiles = range(start // 128, 2)
        lane0 = tiles[0] * 128
        lane = lax.broadcasted_iota(I32, (QUAD, 256 - lane0), 1)
        here = [slice((start + i) * QUAD, (start + i + 1) * QUAD) for i in range(PANEL)]
        rows = [jnp.concatenate([work_ref[t, at, :] for t in tiles], axis=1) for at in here]
        for k in range(PANEL):
            at = start + k - lane0
            head = rows[k]
            pivot = head[:, at : at + 1]
            scaled = head * (1.0 / pivot)
            for i in range(k + 1, PANEL):
                rows[i] = rows[i] - head[:, at + i - k : at + i - k + 1] * scaled
            done = jnp.where(lane >= at, head * (1.0 / jnp.sqrt(pivot)), 0.0)
            for t in tiles:
                panel_ref[t, k * QUAD : (k + 1) * QUAD, :] = done[:, t * 128 - lane0 : t * 128 - lane0 + 128]
        after = start + PANEL
        for m in range(QUAD):
            panel = jnp.concatenate([panel_ref[t, rows_of(m, 0, PANEL), :] for t in tiles], axis=1)
            done = panel[:, : 192 - lane0]
            out_ref[m, start:after, :] = done if lane0 == 0 else jnp.concatenate([zeros(PANEL, lane0), done], axis=1)
            if after < 192:
                update = square(panel)[after - lane0 : 192 - lane0, :]
                rest = rows_of(m, after, 192 - after)
                for t in tiles:
                    work_ref[t, rest, :] = work_ref[t, rest, :] - update[:, t * 128 - lane0 : t * 128 - lane0 + 128]


def reduce_kernel(gram_ref, out_ref, pair_ref, sum_ref, part_ref, relay_ref, work_ref, panel_ref,
                  pair_send, pair_recv, ring_send, ring_recv):
    sky, tm = lax.axis_index("sky"), lax.axis_index("tm")
    z, core = tm // 2, lax.rem(tm, 2)
    up, down, far = lax.rem(z + 1, 4), lax.rem(z + 3, 4), lax.rem(z + 2, 4)
    partner = (sky, z * 2 + 1 - core)
    above, below = (sky, up * 2 + core), (sky, down * 2 + core)

    barrier = pltpu.get_barrier_semaphore()
    for other in (partner, above, below):
        pl.semaphore_signal(barrier, inc=1, device_id=other, device_id_type=MESH)
    pl.semaphore_wait(barrier, 3)

    pairs = []
    for n, at in enumerate((far, up, down, z)):
        copy = pltpu.make_async_remote_copy(
            src_ref=gram_ref.at[at * 2 + 1 - core], dst_ref=pair_ref.at[at],
            send_sem=pair_send.at[n], recv_sem=pair_recv.at[n], device_id=partner, device_id_type=MESH,
        )
        copy.start()
        pairs.append(copy)

    def join_pair(n, at):
        pairs[n].wait_recv()
        sum_ref[at] = gram_ref[at * 2 + core] + pair_ref[at]

    def ring(n, src, to):
        copy = pltpu.make_async_remote_copy(
            src_ref=src, dst_ref=part_ref.at[n],
            send_sem=ring_send.at[n], recv_sem=ring_recv.at[n], device_id=to, device_id_type=MESH,
        )
        copy.start()
        return copy

    first, second = pl.ds(0, 2), pl.ds(2, 2)
    join_pair(0, far)
    far_up = ring(0, sum_ref.at[far, first], above)
    far_down = ring(1, sum_ref.at[far, second], below)
    join_pair(1, up)
    near_up = ring(2, sum_ref.at[up, second], above)
    join_pair(2, down)
    near_down = ring(3, sum_ref.at[down, first], below)
    far_up.wait_recv()
    relay_ref[0] = part_ref[0] + sum_ref[up, 0:2]
    last_up = ring(4, relay_ref.at[0], above)
    far_down.wait_recv()
    relay_ref[1] = part_ref[1] + sum_ref[down, 2:4]
    last_down = ring(5, relay_ref.at[1], below)
    join_pair(3, z)
    near_down.wait_recv()
    near_up.wait_recv()
    sum_ref[z, 0:2] = sum_ref[z, 0:2] + part_ref[3]
    sum_ref[z, 2:4] = sum_ref[z, 2:4] + part_ref[2]
    last_up.wait_recv()
    last_down.wait_recv()
    total = jnp.concatenate([sum_ref[z, 0:2] + part_ref[4], sum_ref[z, 2:4] + part_ref[5]], axis=0)
    for copy in (*pairs, far_up, far_down, near_up, near_down, last_up, last_down):
        copy.wait_send()
    factor(total, out_ref, work_ref, panel_ref)


def reduce_factor(gram):
    vmem = pl.BlockSpec(memory_space=pltpu.VMEM)
    return pl.pallas_call(
        reduce_kernel,
        out_shape=jax.ShapeDtypeStruct((QUAD, 192, 192), F32),
        in_specs=[vmem],
        out_specs=vmem,
        scratch_shapes=[
            pltpu.VMEM((4, QUAD, COEFFS, 384), F32),
            pltpu.VMEM((4, QUAD, COEFFS, 384), F32),
            pltpu.VMEM((6, 2, COEFFS, 384), F32),
            pltpu.VMEM((2, 2, COEFFS, 384), F32),
            pltpu.VMEM((2, 192 * QUAD, 128), F32),
            pltpu.VMEM((2, PANEL * QUAD, 128), F32),
            pltpu.SemaphoreType.DMA((4,)),
            pltpu.SemaphoreType.DMA((4,)),
            pltpu.SemaphoreType.DMA((6,)),
            pltpu.SemaphoreType.DMA((6,)),
        ],
        compiler_params=pltpu.CompilerParams(collective_id=1, has_side_effects=True),
        name="reduce_factor",
    )(gram.reshape(TM, QUAD, COEFFS, 384))


def per_device(reference_spectra, observed, epoch_time, owner, source_row, unit):
    obs = observed[0].T
    times = epoch_time.reshape(128, 128)
    owners = owner.reshape(128, 128)
    rows = source_row.reshape(128, 128)
    units = unit.reshape(128, 128)
    scale = UNITS / (E_DEV * TM)
    number = jnp.zeros((1,), I32)
    table, *plan = prepare(number, owners, rows, units, reference_spectra.T)

    replies, more, local = exchange(0, plan, table, times, obs)
    gram = join(plan, replies, local, scale)

    def next_round(state):
        number, _, gram = state
        number = number + 1
        plan = route(number, owners, rows, units)
        replies, more, local = exchange(3, plan, table, times, obs)
        return number, more, join(plan, replies, local, scale, gram)

    gram = lax.while_loop(lambda state: state[1][0, 0] > 0, next_round, (number, more, gram))[2]
    return reduce_factor(gram)[None]


def solution(mesh):
    placed = (
        P("sky", None),
        P("sky", "tm", None),
        P("sky", "tm"),
        P("sky", "tm", None),
        P("sky", "tm"),
        P("sky", "tm", None),
    )
    return jax.shard_map(
        per_device,
        mesh=mesh,
        in_specs=placed,
        out_specs=P("sky", "tm", None, None),
        check_vma=False,
    )
```
